768 devices in a mesh: lat: 4 (over x_lo, core), lon: 12 (over z), ch: 16 (over y, x_hi).
Axes of the slice: x: 4 (x_hi: 2, x_lo: 2; x = x_hi * 2 + x_lo), y: 8, z: 12, core: 2. Of those that a mesh axis runs over, the one named last changes fastest.
Arguments:
- state_field: bfloat16 [256, 64, 3072], P('ch', 'lat', 'lon'), may hold values from -6 to 6
- land_mask: int32 [64, 3072], P('lat', 'lon'), may hold values 0 or 1
- partner: int32 [3072], replicated, may hold values from 0 to 3071, as said below
- kernel: bfloat16 [256, 49], P('ch'), may hold values from -0.875 to 0.875
- w_expand: bfloat16 [256, 1024], P(None, 'ch'), may hold values from -0.5 to 0.5
- w_project: bfloat16 [1024, 256], P('ch'), may hold values from -0.25 to 0.25
- cotangent: bfloat16 [256, 64, 3072], P('ch', 'lat', 'lon'), may hold values from -6 to 6
Outputs:
- state_out: bfloat16 [256, 64, 3072], P('ch', 'lat', 'lon')
- state_grad: bfloat16 [256, 64, 3072], P('ch', 'lat', 'lon')
The draws below stay inside these ranges and needn't reach their ends.
Inputs may be any that keep to these rules, and one draw needn't show every extreme that they name: partner[i] = (s - i) mod 3072 for one s of the draw, so a column's partner's partner is the column itself.
All inputs are finite; a program needn't handle non-finite values. No bound on the sum of `land_mask` on one device may be relied on, other than what follows from the above.
Results may differ from the reference program's by a relative error of at most 0.017.
Values may be sent and summed in bfloat16 or wider, within the bound.
A program may use at most 64 MiB of HBM per device.

```python
import jax
import jax.numpy as jnp
from jax import lax

C = 256
F = 1024
HB = 16
WB = 256
NH = 64
NW = 3072
N_CH = 16


def draw_partner(key, part):
    pivot = jax.random.randint(key, (), 0, NW, dtype=jnp.int32)
    return jnp.mod(pivot - jnp.arange(NW, dtype=jnp.int32), NW).astype(jnp.int32)


def with_ends(array, own_key, least, top_value):
    longest = array.shape.index(max(array.shape))
    spots = []
    for shift in (0, 1):
        where = [jax.random.randint(jax.random.fold_in(own_key, axis), (), 0, length) for axis, length in enumerate(array.shape)]
        where[longest] = (where[longest] + shift) % array.shape[longest]
        spots.append(tuple(where))
    return array.at[spots[0]].set(least).at[spots[1]].set(top_value)


def raised(entries, stream_key, source, target, parts, factor):
    owner, partner = [(jnp.arange(entries.shape[position]) // (entries.shape[position] // parts)).reshape([-1 if axis == position else 1 for axis in range(entries.ndim)]) for position in (source, target)]
    chosen = jax.random.permutation(stream_key, parts)[partner]
    strong = (owner == chosen) | (owner == (partner + parts // 2) % parts)
    return jnp.where(strong, factor * entries, entries)


def level_of(rng, extent, shards, smallest, largest):
    gain = 1.0
    for dim, blocks in shards:
        draws = jax.random.uniform(jax.random.fold_in(jax.random.fold_in(rng, 6), dim), (blocks,), jnp.float32, smallest / len(shards), largest / len(shards))
        gain = gain * jnp.repeat(jnp.exp(draws), extent[dim] // blocks).reshape((-1,) + (1,) * (len(extent) - 1 - dim))
    return gain


def gaussian(own_key, dims, deviation, most, pieces=(), kind=jnp.bfloat16):
    gain = level_of(own_key, dims, pieces, -0.22, 0.18) if pieces else 1.0
    array = jax.random.normal(own_key, dims, jnp.float32) * deviation * gain
    return jnp.minimum(jnp.maximum(array, -most), most).astype(kind)


def heavy_noise(rng, dims, scale, most, cuts, heavy, kind=jnp.bfloat16):
    result = scale * jax.random.normal(rng, dims, jnp.float32)
    if cuts:
        result = result * level_of(rng, dims, cuts, -0.22, 0.18)
    return jnp.clip(raised(result, jax.random.fold_in(rng, 3), *heavy), -most, most).astype(kind)


def setup_inputs(seed: int = 0) -> dict:
    splits = jax.random.split(jax.random.key(seed), 8)
    return {
        "state_field": gaussian(splits[0], (C, NH, NW), 1.0, 6.0, ((0, 16), (1, 4), (2, 12))),
        "land_mask": with_ends((jax.random.randint(splits[1], (NH, NW), 0, 3) < 2).astype(jnp.int32), jax.random.fold_in(splits[1], 1), 0, 1),
        "partner": draw_partner(jax.random.fold_in(splits[7], 71), 0),
        "kernel": gaussian(splits[3], (C, 49), 49 ** -0.5, 0.875, ((0, 16),)),
        "w_expand": heavy_noise(splits[4], (C, F), C ** -0.5, 0.5, ((1, 16),), (1, 0, 16, 2.0)),
        "w_project": heavy_noise(splits[5], (F, C), F ** -0.5, 0.25, ((0, 16),), (0, 1, 16, 2.0)),
        "cotangent": gaussian(splits[6], (C, NH, NW), 1.0, 6.0, ((0, 16), (1, 4), (2, 12))),
    }


EPSILON = 1e-06

def conv_taps(padded, kernel, out_rows, out_cols):
    running = jnp.zeros((padded.shape[0], out_rows, out_cols), jnp.float32)
    weight_tensors = kernel.astype(jnp.float32)
    for offset in range(49):
        row_off = offset // 7
        col_off = offset % 7
        window = padded[:, row_off:row_off + out_rows, col_off:col_off + out_cols].astype(jnp.float32)
        running = running + weight_tensors[:, offset][:, None, None] * window
    return running

def fold_band(values, partner):
    full_width = values.shape[2]
    top_rows = values[:, values.shape[1] - 3:, :][:, ::-1, :]
    columns = jnp.mod(jnp.arange(-3, full_width + 3, dtype=jnp.int32), full_width)
    return jnp.take(top_rows, partner[columns], axis=2)

def extend(values, partner):
    wrapped = jnp.concatenate([values[:, :, -3:], values, values[:, :, :3]], axis=2)
    south_rows = jnp.zeros((values.shape[0], 3, wrapped.shape[2]), values.dtype)
    return jnp.concatenate([south_rows, wrapped, fold_band(values, partner)], axis=1)

def stencil(values, kernel, partner):
    return conv_taps(extend(values, partner), kernel, values.shape[1], values.shape[2])

def gelu_parts(hidden):
    normal_cdf = 0.5 * (1.0 + lax.erf(hidden * 0.7071067811865476))
    return (hidden * normal_cdf, normal_cdf + hidden * jnp.exp(-0.5 * hidden * hidden) * 0.3989422804014327)

def norm_stats(depth_half):
    values = depth_half.astype(jnp.float32)
    centre = lax.optimization_barrier(jnp.mean(values, axis=0, keepdims=True))
    spread = values - centre
    inv_scale = lax.rsqrt(lax.optimization_barrier(jnp.mean(spread * spread, axis=0, keepdims=True)) + EPSILON)
    return (spread * inv_scale, inv_scale)

def norm_back(partial_value, normed, inv_scale, over_axis):
    mean_plain = lax.optimization_barrier(jnp.mean(partial_value, axis=over_axis, keepdims=True))
    mean_cross = lax.optimization_barrier(jnp.mean(partial_value * normed, axis=over_axis, keepdims=True))
    return inv_scale * (partial_value - mean_plain - normed * mean_cross)

def reference(state_field, land_mask, partner, kernel, w_expand, w_project, cotangent):
    ocean_mask = land_mask.astype(jnp.float32)
    masked = state_field * land_mask.astype(jnp.bfloat16)
    depth_full, conv_back = jax.vjp(lambda values: stencil(values, kernel, partner), masked.astype(jnp.float32))
    depth_half = depth_full.astype(jnp.bfloat16)
    masked_cot = cotangent * land_mask.astype(jnp.bfloat16)
    channels_all = state_field.shape[0]
    row_total = state_field.shape[1]
    col_total = state_field.shape[2]
    block_size = HB * WB
    block_count = row_total * col_total // block_size
    depth_blocks = depth_half.reshape(channels_all, block_count, block_size).transpose(1, 0, 2)
    cot_blocks = masked_cot.reshape(channels_all, block_count, block_size).transpose(1, 0, 2)
    channel_groups = N_CH
    width_per_group = w_project.shape[0] // channel_groups
    projection_groups = w_project.astype(jnp.float32).reshape(channel_groups, width_per_group, channels_all)
    expand_groups = w_expand.astype(jnp.float32).reshape(channels_all, channel_groups, width_per_group)

    def one_block(paired_blocks):
        depth_block, cot_block = paired_blocks
        normed, inv_scale = norm_stats(depth_block)
        hidden = lax.dot_general(w_expand, normed.astype(jnp.bfloat16), (((0,), (0,)), ((), ())), preferred_element_type=jnp.float32)
        active, slope_term = gelu_parts(hidden)
        active_portion = active.astype(jnp.bfloat16)
        output_piece = jnp.einsum('rxj,rxm->rmj', active_portion.astype(jnp.float32).reshape(channel_groups, width_per_group, -1), projection_groups)
        mixed_block = lax.optimization_barrier(jnp.sum(output_piece.astype(jnp.bfloat16).astype(jnp.float32), axis=0))
        back_hidden = (jnp.dot(w_project, cot_block, preferred_element_type=jnp.float32) * slope_term).astype(jnp.bfloat16)
        partial_norm = jnp.einsum('gfn,cgf->gcn', back_hidden.astype(jnp.float32).reshape(channel_groups, width_per_group, -1), expand_groups)
        gradient_piece = norm_back(partial_norm, normed[None], inv_scale[None], 1)
        grad_block = lax.optimization_barrier(jnp.sum(gradient_piece.astype(jnp.bfloat16).astype(jnp.float32), axis=0))
        return (mixed_block, grad_block)
    mixed_all, grad_all = lax.map(one_block, (depth_blocks, cot_blocks))
    mixed = mixed_all.transpose(1, 0, 2).reshape(channels_all, row_total, col_total)
    grad_depth = grad_all.transpose(1, 0, 2).reshape(channels_all, row_total, col_total).astype(jnp.bfloat16)
    state_out = (ocean_mask * (state_field.astype(jnp.float32) + mixed)).astype(jnp.bfloat16)
    grad_masked = conv_back(grad_depth.astype(jnp.float32))[0]
    state_grad = (masked_cot.astype(jnp.float32) + ocean_mask * grad_masked).astype(jnp.bfloat16)
    return (state_out, state_grad)
```

```python
import jax
import jax.numpy as jnp
from jax import lax
from jax.sharding import PartitionSpec as P

EPSILON = 1e-06


def with_halo(value, sides, width):
    for axis, dim in sides:
        count, length = (lax.axis_size(axis), value.shape[dim])
        up = [(i, (i + 1) % count) for i in range(count)]
        down = [(j, i) for i, j in up]
        last = lax.slice_in_dim(value, length - width, length, axis=dim)
        first = lax.slice_in_dim(value, 0, width, axis=dim)
        before = lax.ppermute(last, axis, up)
        after = lax.ppermute(first, axis, down)
        value = jnp.concatenate([before, value, after], axis=dim)
    return value


def conv_taps(padded, kernel, out_rows, out_cols):
    running = jnp.zeros((padded.shape[0], out_rows, out_cols), jnp.float32)
    weight_tensors = kernel.astype(jnp.float32)
    for offset in range(49):
        row_off = offset // 7
        col_off = offset % 7
        window = padded[:, row_off : row_off + out_rows, col_off : col_off + out_cols].astype(
            jnp.float32
        )
        running = running + weight_tensors[:, offset][:, None, None] * window
    return running


def gelu_parts(hidden):
    normal_cdf = 0.5 * (1.0 + lax.erf(hidden * 0.7071067811865476))
    return (
        hidden * normal_cdf,
        normal_cdf + hidden * jnp.exp(-0.5 * hidden * hidden) * 0.3989422804014327,
    )


def norm_stats(depth_half):
    values = depth_half.astype(jnp.float32)
    centre = jnp.mean(values, axis=0, keepdims=True)
    spread = values - centre
    inv_scale = lax.rsqrt(jnp.mean(spread * spread, axis=0, keepdims=True) + EPSILON)
    return (spread * inv_scale, inv_scale)


def norm_back(partial_value, normed, inv_scale, over_axis):
    mean_plain = jnp.mean(partial_value, axis=over_axis, keepdims=True)
    mean_cross = jnp.mean(partial_value * normed, axis=over_axis, keepdims=True)
    return inv_scale * (partial_value - mean_plain - normed * mean_cross)


def on_device(state_field, land_mask, partner, kernel, w_expand, w_project, cotangent):
    channels_here, row_count, col_count = state_field.shape
    full_width = partner.shape[0]
    cell_count = row_count * col_count
    lat_last = lax.axis_index("lat") == lax.axis_size("lat") - 1
    lat_first = lax.axis_index("lat") == 0
    lon_start = lax.axis_index("lon") * col_count
    ocean_mask = land_mask.astype(jnp.float32)
    masked = state_field * land_mask.astype(jnp.bfloat16)
    row_ids = jnp.arange(row_count + 6)
    row_keep = jnp.logical_not(lat_first & (row_ids < 3) | lat_last & (row_ids >= row_count + 3))
    top_flag = lat_last.astype(jnp.bfloat16)
    fold_columns = partner[
        jnp.mod(lon_start + jnp.arange(-3, col_count + 3, dtype=jnp.int32), full_width)
    ]

    def with_rims(values):
        padded = with_halo(values, (("lat", 1), ("lon", 2)), 3)
        return padded * row_keep[None, :, None].astype(values.dtype)

    def fold_band(values):
        gathered = lax.all_gather(values[:, row_count - 3 :, :], "lon", axis=2, tiled=True)
        return jnp.take(gathered[:, ::-1, :], fold_columns, axis=2) * top_flag

    padded = with_rims(masked)
    padded = jnp.concatenate(
        [padded[:, : row_count + 3], padded[:, row_count + 3 :] + fold_band(masked)], axis=1
    )
    depth_half = conv_taps(padded, kernel, row_count, col_count).astype(jnp.bfloat16)
    masked_cot = cotangent * land_mask.astype(jnp.bfloat16)
    expand_all = lax.all_gather(w_expand, "ch", axis=1, tiled=True)
    project_all = lax.all_gather(w_project, "ch", axis=0, tiled=True)
    full_depth = lax.all_to_all(depth_half, "ch", 1, 0, tiled=True).reshape(-1, col_count)
    full_cot = lax.all_to_all(masked_cot, "ch", 1, 0, tiled=True).reshape(-1, col_count)
    normed, inv_scale = norm_stats(full_depth)
    hidden = lax.dot_general(
        expand_all,
        normed.astype(jnp.bfloat16),
        (((0,), (0,)), ((), ())),
        preferred_element_type=jnp.float32,
    )
    active, slope_term = gelu_parts(hidden)
    mixed_rows = lax.dot_general(
        project_all,
        active.astype(jnp.bfloat16),
        (((0,), (0,)), ((), ())),
        preferred_element_type=jnp.float32,
    ).astype(jnp.bfloat16)
    back_hidden = (
        jnp.dot(project_all, full_cot, preferred_element_type=jnp.float32) * slope_term
    ).astype(jnp.bfloat16)
    full_norm = jnp.dot(expand_all, back_hidden, preferred_element_type=jnp.float32)
    grad_rows = norm_back(full_norm, normed, inv_scale, 0).astype(jnp.bfloat16)
    mixed = lax.all_to_all(mixed_rows[:, None, :], "ch", 0, 1, tiled=True).astype(jnp.float32)
    grad_depth = lax.all_to_all(grad_rows[:, None, :], "ch", 0, 1, tiled=True)
    state_out = (ocean_mask * (state_field.astype(jnp.float32) + mixed)).astype(jnp.bfloat16)
    flipped = kernel.reshape(channels_here, 7, 7)[:, ::-1, ::-1].reshape(channels_here, 49)
    grad_masked = conv_taps(with_rims(grad_depth), flipped, row_count, col_count)
    folded = jnp.concatenate(
        [jnp.zeros((channels_here, 6, col_count + 6), jnp.bfloat16), fold_band(grad_depth)], axis=1
    )
    top_part = conv_taps(folded, kernel, 3, col_count)
    grad_masked = jnp.concatenate(
        [grad_masked[:, : row_count - 3], grad_masked[:, row_count - 3 :] + top_part], axis=1
    )
    state_grad = (masked_cot.astype(jnp.float32) + ocean_mask * grad_masked).astype(jnp.bfloat16)
    return (state_out, state_grad)


def solution(mesh):
    placed = (
        P("ch", "lat", "lon"),
        P("lat", "lon"),
        P(),
        P("ch", None),
        P(None, "ch"),
        P("ch", None),
        P("ch", "lat", "lon"),
    )
    return jax.shard_map(
        on_device,
        mesh=mesh,
        in_specs=placed,
        out_specs=(P("ch", "lat", "lon"), P("ch", "lat", "lon")),
        check_vma=False,
    )
```

```python
import functools

import jax
import jax.numpy as jnp
from jax import lax
from jax.experimental import pallas as pl
from jax.experimental.pallas import tpu as pltpu
from jax.sharding import PartitionSpec as P

EPSILON = 1e-06
HALO = 3
EDGE = 128
TAPS = 7
DIRECTIONS = ((-1, 0), (1, 0), (0, -1), (0, 1), (-1, -1), (-1, 1), (1, -1), (1, 1))
MESH = pl.DeviceIdType.MESH
F32 = jnp.float32
BF16 = jnp.bfloat16


def dot(a, b, dims=((1,), (0,))):
    return lax.dot_general(a, b, (dims, ((), ())), preferred_element_type=F32)


def gelu_parts(hidden):
    normal_cdf = 0.5 * (1.0 + lax.erf(hidden * 0.7071067811865476))
    return (
        hidden * normal_cdf,
        normal_cdf + hidden * jnp.exp(-0.5 * hidden * hidden) * 0.3989422804014327,
    )


def block_kernel(
    sizes,
    partner_ref,
    state_ref,
    mask_ref,
    kernel_ref,
    expand_ref,
    project_ref,
    cot_ref,
    out_ref,
    grad_ref,
    ext,
    ext_back,
    fold_rows,
    fold_rows_back,
    pick,
    taps,
    acc,
    cot_rows,
    cot_all,
    depth_rows,
    depth_all,
    weights,
    normed_ref,
    mixed_send,
    grad_send,
    mixed_rows,
    halo_send,
    halo_recv,
    halo_send_back,
    halo_recv_back,
    send,
    recv,
):
    n_lat, n_lon, n_ch, rows, chans, cols, hidden_here = sizes
    wide = cols + 2 * EDGE
    cells = rows * chans
    lat, lon, me = lax.axis_index("lat"), lax.axis_index("lon"), lax.axis_index("ch")
    lat_last = lat == n_lat - 1
    part = lax.rem(lat, 2)
    sibling = lat + 1 - 2 * part
    own_rows = pl.ds(HALO, rows)
    own_lanes = pl.ds(EDGE, cols)

    def exists(dl):
        return jnp.logical_and(lat + dl >= 0, lat + dl < n_lat)

    def at(dl, do):
        return {"lat": lat + dl, "lon": lax.rem(lon + do + n_lon, n_lon), "ch": me}

    barrier = pltpu.get_barrier_semaphore()

    def greet_channel(i, carry):
        pl.semaphore_signal(
            barrier,
            device_id={"lat": lat, "lon": lon, "ch": lax.rem(me + i, n_ch)},
            device_id_type=MESH,
        )
        return carry

    def greet_fold(i, carry):
        pl.semaphore_signal(
            barrier,
            device_id={"lat": lat, "lon": lax.rem(lon + i, n_lon), "ch": me},
            device_id_type=MESH,
        )
        return carry

    for dl, do in DIRECTIONS:

        @pl.when(exists(dl))
        def _():
            pl.semaphore_signal(barrier, device_id=at(dl, do), device_id_type=MESH)

    lax.fori_loop(1, n_ch, greet_channel, 0)

    @pl.when(lat_last)
    def _():
        lax.fori_loop(1, n_lon, greet_fold, 0)

    swap_row = lax.broadcasted_iota(jnp.int32, (cells, cells), 0)
    swap_col = lax.broadcasted_iota(jnp.int32, (cells, cells), 1)
    to_rows = (swap_col == lax.rem(swap_row, chans) * rows + swap_row // chans).astype(BF16)
    mask_half = mask_ref[...].astype(BF16)
    masked = (state_ref[...] * mask_half[None]).reshape(cells, cols)
    ext[own_rows, :, own_lanes] = (
        dot(to_rows, masked).astype(BF16).reshape(rows, chans, cols)
    )
    masked_cot = (cot_ref[...] * mask_half[None]).reshape(cells, cols)
    cot_rows[...] = dot(to_rows, masked_cot).astype(BF16).reshape(rows, chans, cols)
    cot_all[me] = cot_rows[me]

    @pl.when(part == 0)
    def _():
        unit_row = lax.broadcasted_iota(jnp.int32, (n_ch * chans, n_ch * chans), 0)
        unit_col = lax.broadcasted_iota(jnp.int32, (n_ch * chans, n_ch * chans), 1)
        unit = (unit_row == unit_col).astype(BF16)
        weights[0, me] = dot(expand_ref[...], unit, ((0,), (0,))).astype(BF16)

    @pl.when(part == 1)
    def _():
        weights[1, me] = project_ref[...]

    for t in range(TAPS * TAPS):
        tap = jnp.broadcast_to(kernel_ref[:, t : t + 1].astype(F32), (chans, EDGE))
        taps[0, t] = tap
        taps[1, TAPS * TAPS - 1 - t] = tap

    @pl.when(lat == 0)
    def _():
        ext[0:HALO] = jnp.zeros((HALO, chans, wide), BF16)
        ext_back[0:HALO] = jnp.zeros((HALO, chans, wide), BF16)

    @pl.when(lat_last)
    def _():
        fold_rows[lon] = ext[pl.ds(rows, HALO), :, own_lanes]

    neighbours = sum(
        (exists(dl).astype(jnp.int32) for dl, _ in DIRECTIONS), jnp.int32(n_ch - 1)
    ) + jnp.where(lat_last, n_lon - 1, 0)
    pl.semaphore_wait(barrier, neighbours)

    def halo_copy(buffer, d, send_sems, recv_sems):
        dl, do = DIRECTIONS[d]
        src_rows, dst_rows = {
            -1: (pl.ds(HALO, HALO), pl.ds(HALO + rows, HALO)),
            0: (own_rows, own_rows),
            1: (pl.ds(rows, HALO), pl.ds(0, HALO)),
        }[dl]
        src_lanes, dst_lanes = {
            -1: (pl.ds(EDGE, EDGE), pl.ds(EDGE + cols, EDGE)),
            0: (own_lanes, own_lanes),
            1: (pl.ds(cols, EDGE), pl.ds(0, EDGE)),
        }[do]
        return pltpu.make_async_remote_copy(
            src_ref=buffer.at[src_rows, :, src_lanes],
            dst_ref=buffer.at[dst_rows, :, dst_lanes],
            send_sem=send_sems.at[d],
            recv_sem=recv_sems.at[d],
            device_id=at(dl, do),
            device_id_type=MESH,
        )

    def halo_start(buffer, send_sems, recv_sems):
        for d, (dl, _) in enumerate(DIRECTIONS):
            pl.when(exists(dl))(lambda d=d: halo_copy(buffer, d, send_sems, recv_sems).start())

    def halo_arrived(buffer, send_sems, recv_sems):
        for d, (dl, _) in enumerate(DIRECTIONS):
            pl.when(exists(-dl))(
                lambda d=d: halo_copy(buffer, d, send_sems, recv_sems).wait_recv()
            )

    def halo_sent(buffer, send_sems, recv_sems):
        for d, (dl, _) in enumerate(DIRECTIONS):
            pl.when(exists(dl))(
                lambda d=d: halo_copy(buffer, d, send_sems, recv_sems).wait_send()
            )

    def fold_copy(buffer, gathered, i, k):
        return pltpu.make_async_remote_copy(
            src_ref=buffer.at[pl.ds(rows, HALO), :, own_lanes],
            dst_ref=gathered.at[lon],
            send_sem=send.at[k],
            recv_sem=recv.at[k],
            device_id={"lat": lat, "lon": lax.rem(lon + i, n_lon), "ch": me},
            device_id_type=MESH,
        )

    def several(gathered, count, k):
        whole = gathered.at[pl.ds(0, count)]
        return pltpu.make_async_remote_copy(
            src_ref=whole,
            dst_ref=whole,
            send_sem=send.at[k],
            recv_sem=recv.at[k],
            device_id={"lat": lat, "lon": lon, "ch": lax.rem(me + 1, n_ch)},
            device_id_type=MESH,
        )

    def channel_copies(make_src, make_dst, k):
        def step(i, carry):
            peer = lax.rem(me + i, n_ch)
            pltpu.make_async_remote_copy(
                src_ref=make_src(peer),
                dst_ref=make_dst(),
                send_sem=send.at[k],
                recv_sem=recv.at[k],
                device_id={"lat": lat, "lon": lon, "ch": peer},
                device_id_type=MESH,
            ).start()
            return carry

        lax.fori_loop(1, n_ch, step, 0)

    def fold_start(buffer, gathered, k):
        def step(i, carry):
            fold_copy(buffer, gathered, i, k).start()
            return carry

        lax.fori_loop(1, n_lon, step, 0)

    halo_start(ext, halo_send, halo_recv)

    @pl.when(lat_last)
    def _():
        fold_start(ext, fold_rows, 0)

    own_weights = weights.at[part, me]
    channel_copies(lambda peer: own_weights, lambda: own_weights, 1)
    channel_copies(lambda peer: cot_rows.at[peer], lambda: cot_all.at[me], 2)

    full_width = n_lon * cols
    turn = partner_ref[0]
    first = lax.rem(turn - lon * cols - (cols + HALO - 1) + 2 * full_width, full_width)
    first_block = first // cols
    origin = lax.rem(turn - lon * cols + EDGE - first_block * cols + 3 * full_width, full_width)

    @pl.when(lat_last)
    def _():
        source = lax.broadcasted_iota(jnp.int32, (3 * cols, wide), 0)
        want = origin - lax.broadcasted_iota(jnp.int32, (3 * cols, wide), 1)
        want = jnp.where(want < 0, want + full_width, want)
        pick[...] = (source == want).astype(BF16)

    def fold_fill(buffer, gathered):
        found = jnp.zeros((HALO * chans, wide), F32)
        for j in range(3):
            piece = gathered[lax.rem(first_block + j, n_lon)].reshape(HALO * chans, cols)
            found = found + dot(piece, pick[j * cols : (j + 1) * cols, :])
        found = found.astype(BF16).reshape(HALO, chans, wide)
        for j in range(HALO):
            buffer[HALO + rows + j] = found[HALO - 1 - j]

    def conv(buffer, table_of):
        acc[...] = jnp.zeros(acc.shape, F32)

        def step(e, carry):
            table = table_of(e)
            line = buffer[e].astype(F32)
            shifted = [
                line[:, EDGE - HALO + b : EDGE - HALO + b + cols] for b in range(TAPS)
            ]
            for a in range(TAPS):
                total = acc[e - a + TAPS - 1]
                for b in range(TAPS):
                    tap = taps[table, a * TAPS + b]
                    total = total + jnp.concatenate([tap] * (cols // EDGE), axis=1) * shifted[b]
                acc[e - a + TAPS - 1] = total
            return carry

        lax.fori_loop(0, rows + 2 * HALO, step, 0)

    halo_arrived(ext, halo_send, halo_recv)

    @pl.when(lat_last)
    def _():
        several(fold_rows, n_lon - 1, 0).wait_recv()
        fold_fill(ext, fold_rows)

    conv(ext, lambda e: 0)
    depth_rows[...] = acc[pl.ds(TAPS - 1, rows)].astype(BF16)
    channel_copies(lambda peer: depth_rows.at[peer], lambda: depth_all.at[me], 3)
    depth_all[me] = depth_rows[me]

    def swap_weights():
        return pltpu.make_async_remote_copy(
            src_ref=weights.at[part],
            dst_ref=weights.at[part],
            send_sem=send.at[4],
            recv_sem=recv.at[4],
            device_id={"lat": sibling, "lon": lon, "ch": me},
            device_id_type=MESH,
        )

    several(weights.at[part], n_ch - 1, 1).wait_recv()
    swap_weights().start()
    several(cot_all, n_ch - 1, 2).wait_recv()
    several(depth_all, n_ch - 1, 3).wait_recv()

    channels = n_ch * chans
    values = depth_all[...].reshape(channels, cols).astype(F32)
    spread = values - jnp.mean(values, axis=0, keepdims=True)
    inv_scale = lax.rsqrt(jnp.mean(spread * spread, axis=0, keepdims=True) + EPSILON)
    normed_ref[...] = spread * inv_scale
    normed_half = normed_ref[...].astype(BF16)
    cot_here = cot_all[...].reshape(channels, cols)
    pltpu.make_async_remote_copy(
        src_ref=weights.at[1 - part],
        dst_ref=weights.at[1 - part],
        send_sem=send.at[4],
        recv_sem=recv.at[4],
        device_id={"lat": sibling, "lon": lon, "ch": me},
        device_id_type=MESH,
    ).wait_recv()

    mixed = jnp.zeros((channels, cols), F32)
    back_norm = jnp.zeros((channels, cols), F32)
    per_chunk = n_ch // 4
    for j in range(4):
        span = slice(j * per_chunk, (j + 1) * per_chunk)
        expand = weights[0, span].reshape(per_chunk * hidden_here, channels)
        project = weights[1, span].reshape(per_chunk * hidden_here, channels)
        active, slope = gelu_parts(dot(expand, normed_half))
        back_hidden = (dot(project, cot_here) * slope).astype(BF16)
        mixed = mixed + dot(project, active.astype(BF16), ((0,), (0,)))
        back_norm = back_norm + dot(expand, back_hidden, ((0,), (0,)))
    normed = normed_ref[...]
    mean_plain = jnp.mean(back_norm, axis=0, keepdims=True)
    mean_cross = jnp.mean(back_norm * normed, axis=0, keepdims=True)
    grad_send[...] = (
        (inv_scale * (back_norm - mean_plain - normed * mean_cross))
        .astype(BF16)
        .reshape(n_ch, chans, cols)
    )
    back_row = ext_back.at[HALO + me, :, own_lanes]
    channel_copies(lambda peer: grad_send.at[peer], lambda: back_row, 5)
    ext_back[HALO + me, :, own_lanes] = grad_send[me]
    mixed_send[...] = mixed.astype(BF16).reshape(n_ch, chans, cols)
    channel_copies(lambda peer: mixed_send.at[peer], lambda: mixed_rows.at[me], 6)
    mixed_rows[me] = mixed_send[me]

    several(grad_send, n_ch - 1, 5).wait_recv()
    halo_start(ext_back, halo_send_back, halo_recv_back)

    @pl.when(lat_last)
    def _():
        fold_start(ext_back, fold_rows_back, 7)
        fold_rows_back[lon] = ext_back[pl.ds(rows, HALO), :, own_lanes]

    several(mixed_rows, n_ch - 1, 6).wait_recv()
    to_chans = (swap_col == lax.rem(swap_row, rows) * chans + swap_row // rows).astype(BF16)
    mixed_here = dot(to_chans, mixed_rows[...].reshape(cells, cols)).reshape(chans, rows, cols)
    ocean = mask_ref[...].astype(F32)
    out_ref[...] = (ocean[None] * (state_ref[...].astype(F32) + mixed_here)).astype(BF16)

    halo_arrived(ext_back, halo_send_back, halo_recv_back)

    @pl.when(lat_last)
    def _():
        several(fold_rows_back, n_lon - 1, 7).wait_recv()
        fold_fill(ext_back, fold_rows_back)

    fold_from = jnp.where(lat_last, HALO + rows, rows + 2 * HALO)
    conv(ext_back, lambda e: jnp.where(e >= fold_from, 0, 1))
    grad_rows = (
        cot_rows[...].astype(F32) + ocean[:, None, :] * acc[pl.ds(TAPS - 1, rows)]
    ).astype(BF16)
    grad_ref[...] = (
        dot(to_chans, grad_rows.reshape(cells, cols)).astype(BF16).reshape(chans, rows, cols)
    )

    halo_sent(ext, halo_send, halo_recv)
    halo_sent(ext_back, halo_send_back, halo_recv_back)

    @pl.when(lat_last)
    def _():
        several(fold_rows, n_lon - 1, 0).wait_send()
        several(fold_rows_back, n_lon - 1, 7).wait_send()

    several(weights.at[part], n_ch - 1, 1).wait_send()
    several(cot_rows, n_ch - 1, 2).wait_send()
    several(depth_rows, n_ch - 1, 3).wait_send()
    swap_weights().wait_send()
    several(grad_send, n_ch - 1, 5).wait_send()
    several(mixed_send, n_ch - 1, 6).wait_send()


def on_device(state_field, land_mask, partner, kernel, w_expand, w_project, cotangent):
    n_lat, n_lon, n_ch = (lax.axis_size(name) for name in ("lat", "lon", "ch"))
    chans, rows, cols = state_field.shape
    hidden_here = w_project.shape[0]
    assert rows == n_ch and n_lat % 2 == 0
    wide = cols + 2 * EDGE
    channels = n_ch * chans
    sizes = (n_lat, n_lon, n_ch, rows, chans, cols, hidden_here)
    vmem = pl.BlockSpec(memory_space=pltpu.VMEM)
    tile_rows = rows + 2 * HALO
    return pl.pallas_call(
        functools.partial(block_kernel, sizes),
        out_shape=(jax.ShapeDtypeStruct(state_field.shape, BF16),) * 2,
        in_specs=[pl.BlockSpec(memory_space=pltpu.SMEM)] + [vmem] * 6,
        out_specs=(vmem, vmem),
        scratch_shapes=[
            pltpu.VMEM((tile_rows, chans, wide), BF16),
            pltpu.VMEM((tile_rows, chans, wide), BF16),
            pltpu.VMEM((n_lon, HALO, chans, cols), BF16),
            pltpu.VMEM((n_lon, HALO, chans, cols), BF16),
            pltpu.VMEM((3 * cols, wide), BF16),
            pltpu.VMEM((2, TAPS * TAPS, chans, EDGE), F32),
            pltpu.VMEM((rows + 2 * (TAPS - 1), chans, cols), F32),
            pltpu.VMEM((rows, chans, cols), BF16),
            pltpu.VMEM((n_ch, chans, cols), BF16),
            pltpu.VMEM((rows, chans, cols), BF16),
            pltpu.VMEM((n_ch, chans, cols), BF16),
            pltpu.VMEM((2, n_ch, hidden_here, channels), BF16),
            pltpu.VMEM((channels, cols), F32),
            pltpu.VMEM((n_ch, chans, cols), BF16),
            pltpu.VMEM((n_ch, chans, cols), BF16),
            pltpu.VMEM((n_ch, chans, cols), BF16),
            pltpu.SemaphoreType.DMA((8,)),
            pltpu.SemaphoreType.DMA((8,)),
            pltpu.SemaphoreType.DMA((8,)),
            pltpu.SemaphoreType.DMA((8,)),
            pltpu.SemaphoreType.DMA((8,)),
            pltpu.SemaphoreType.DMA((8,)),
        ],
        compiler_params=pltpu.CompilerParams(
            collective_id=0, has_side_effects=True, vmem_limit_bytes=48 * 1024 * 1024
        ),
        name="ocean_block",
    )(partner, state_field, land_mask, kernel, w_expand, w_project, cotangent)


def solution(mesh):
    placed = (
        P("ch", "lat", "lon"),
        P("lat", "lon"),
        P(),
        P("ch", None),
        P(None, "ch"),
        P("ch", None),
        P("ch", "lat", "lon"),
    )
    return jax.shard_map(
        on_device,
        mesh=mesh,
        in_specs=placed,
        out_specs=(P("ch", "lat", "lon"), P("ch", "lat", "lon")),
        check_vma=False,
    )
```

```python
import functools

import jax
import jax.numpy as jnp
from jax import lax
from jax.experimental import pallas as pl
from jax.experimental.pallas import tpu as pltpu
from jax.sharding import PartitionSpec as P

EPSILON = 1e-06
HALO = 3
EDGE = 128
TAPS = 7
DIRECTIONS = ((-1, 0), (1, 0), (0, -1), (0, 1), (-1, -1), (-1, 1), (1, -1), (1, 1))
MESH = pl.DeviceIdType.MESH
F32 = jnp.float32
BF16 = jnp.bfloat16


def dot(a, b, dims=((1,), (0,))):
    return lax.dot_general(a, b, (dims, ((), ())), preferred_element_type=F32)


def gelu_parts(hidden):
    normal_cdf = 0.5 * (1.0 + lax.erf(hidden * 0.7071067811865476))
    return (
        hidden * normal_cdf,
        normal_cdf + hidden * jnp.exp(-0.5 * hidden * hidden) * 0.3989422804014327,
    )


def block_kernel(
    sizes,
    partner_hbm,
    state_hbm,
    mask_hbm,
    kernel_hbm,
    expand_hbm,
    project_hbm,
    cot_hbm,
    mixed_rows,
    grad_rows,
    partner_ref,
    state_ref,
    mask_ref,
    kernel_ref,
    cot_ref,
    ext,
    ext_back,
    fold_rows,
    fold_rows_back,
    pick,
    taps,
    acc,
    cot_rows,
    cot_all,
    depth_rows,
    depth_all,
    weights,
    normed_ref,
    mixed_send,
    grad_send,
    halo_send,
    halo_recv,
    halo_send_back,
    halo_recv_back,
    send,
    recv,
    square_send,
    square_recv,
    load,
):
    n_lat, n_lon, n_ch, rows, chans, cols, hidden_here = sizes
    wide = cols + 2 * EDGE
    cells = rows * chans
    lat, lon, me = lax.axis_index("lat"), lax.axis_index("lon"), lax.axis_index("ch")
    lat_last = lat == n_lat - 1
    part = lax.rem(lat, 2)
    sibling = lat + 1 - 2 * part
    pairs = n_lat // 2
    share = hidden_here // (2 * pairs)
    mine = pl.ds(pl.multiple_of((lat // 2 * 2 + lax.rem(lon, 2)) * share, share), share)
    lon_twin = lon + 1 - 2 * lax.rem(lon, 2)
    square = [(0, 1)] + [(2 * i, j) for i in range(1, pairs) for j in (0, 1)]

    def in_square(turn, flip):
        return {
            "lat": lax.rem(lat + turn, n_lat),
            "lon": lon_twin if flip else lon,
            "ch": me,
        }
    own_rows = pl.ds(HALO, rows)
    own_lanes = pl.ds(EDGE, cols)

    def exists(dl):
        return jnp.logical_and(lat + dl >= 0, lat + dl < n_lat)

    def at(dl, do):
        return {"lat": lat + dl, "lon": lax.rem(lon + do + n_lon, n_lon), "ch": me}

    barrier = pltpu.get_barrier_semaphore()

    def greet_channel(i, carry):
        pl.semaphore_signal(
            barrier,
            device_id={"lat": lat, "lon": lon, "ch": lax.rem(me + i, n_ch)},
            device_id_type=MESH,
        )
        return carry

    def greet_fold(i, carry):
        pl.semaphore_signal(
            barrier,
            device_id={"lat": lat, "lon": lax.rem(lon + i, n_lon), "ch": me},
            device_id_type=MESH,
        )
        return carry

    for dl, do in DIRECTIONS:

        @pl.when(exists(dl))
        def _():
            pl.semaphore_signal(barrier, device_id=at(dl, do), device_id_type=MESH)

    lax.fori_loop(1, n_ch, greet_channel, 0)
    for turn, flip in square[1:]:
        pl.semaphore_signal(barrier, device_id=in_square(turn, flip), device_id_type=MESH)

    @pl.when(lat_last)
    def _():
        lax.fori_loop(1, n_lon, greet_fold, 0)

    def fetch(k, src, dst):
        return pltpu.make_async_copy(src, dst, load.at[k])

    loads = [
        fetch(0, state_hbm, state_ref),
        fetch(1, mask_hbm, mask_ref),
        fetch(2, kernel_hbm, kernel_ref),
        fetch(3, cot_hbm, cot_ref),
        fetch(4, partner_hbm, partner_ref),
    ]
    own_expand = fetch(5, expand_hbm.at[mine], weights.at[0, me, mine])
    own_project = fetch(5, project_hbm.at[mine], weights.at[1, me, mine])
    for copy in loads:
        copy.start()

    @pl.when(part == 0)
    def _():
        own_expand.start()

    @pl.when(part == 1)
    def _():
        own_project.start()

    swap_row = lax.broadcasted_iota(jnp.int32, (cells, cells), 0)
    swap_col = lax.broadcasted_iota(jnp.int32, (cells, cells), 1)
    to_rows = (swap_col == lax.rem(swap_row, chans) * rows + swap_row // chans).astype(BF16)
    loads[0].wait()
    loads[1].wait()
    mask_half = mask_ref[...].astype(BF16)
    masked = (state_ref[...] * mask_half[None]).reshape(cells, cols)
    ext[own_rows, :, own_lanes] = (
        dot(to_rows, masked).astype(BF16).reshape(rows, chans, cols)
    )
    @pl.when(lat == 0)
    def _():
        ext[0:HALO] = jnp.zeros((HALO, chans, wide), BF16)
        ext_back[0:HALO] = jnp.zeros((HALO, chans, wide), BF16)

    @pl.when(lat_last)
    def _():
        fold_rows[lon] = ext[pl.ds(rows, HALO), :, own_lanes]

    own_expand.wait()
    neighbours = sum(
        (exists(dl).astype(jnp.int32) for dl, _ in DIRECTIONS), jnp.int32(n_ch - 1 + len(square) - 1)
    ) + jnp.where(lat_last, n_lon - 1, 0)
    pl.semaphore_wait(barrier, neighbours)

    def halo_copy(buffer, d, send_sems, recv_sems):
        dl, do = DIRECTIONS[d]
        src_rows, dst_rows = {
            -1: (pl.ds(HALO, HALO), pl.ds(HALO + rows, HALO)),
            0: (own_rows, own_rows),
            1: (pl.ds(rows, HALO), pl.ds(0, HALO)),
        }[dl]
        src_lanes, dst_lanes = {
            -1: (pl.ds(EDGE, EDGE), pl.ds(EDGE + cols, EDGE)),
            0: (own_lanes, own_lanes),
            1: (pl.ds(cols, EDGE), pl.ds(0, EDGE)),
        }[do]
        return pltpu.make_async_remote_copy(
            src_ref=buffer.at[src_rows, :, src_lanes],
            dst_ref=buffer.at[dst_rows, :, dst_lanes],
            send_sem=send_sems.at[d],
            recv_sem=recv_sems.at[d],
            device_id=at(dl, do),
            device_id_type=MESH,
        )

    def halo_start(buffer, send_sems, recv_sems):
        for d, (dl, _) in enumerate(DIRECTIONS):
            pl.when(exists(dl))(lambda d=d: halo_copy(buffer, d, send_sems, recv_sems).start())

    def halo_arrived(buffer, send_sems, recv_sems):
        for d, (dl, _) in enumerate(DIRECTIONS):
            pl.when(exists(-dl))(
                lambda d=d: halo_copy(buffer, d, send_sems, recv_sems).wait_recv()
            )

    def halo_sent(buffer, send_sems, recv_sems):
        for d, (dl, _) in enumerate(DIRECTIONS):
            pl.when(exists(dl))(
                lambda d=d: halo_copy(buffer, d, send_sems, recv_sems).wait_send()
            )

    def fold_copy(buffer, gathered, i, k):
        return pltpu.make_async_remote_copy(
            src_ref=buffer.at[pl.ds(rows, HALO), :, own_lanes],
            dst_ref=gathered.at[lon],
            send_sem=send.at[k],
            recv_sem=recv.at[k],
            device_id={"lat": lat, "lon": lax.rem(lon + i, n_lon), "ch": me},
            device_id_type=MESH,
        )

    def several(gathered, count, k):
        whole = gathered.at[pl.ds(0, count)]
        return pltpu.make_async_remote_copy(
            src_ref=whole,
            dst_ref=whole,
            send_sem=send.at[k],
            recv_sem=recv.at[k],
            device_id={"lat": lat, "lon": lon, "ch": lax.rem(me + 1, n_ch)},
            device_id_type=MESH,
        )

    def channel_copies(make_src, make_dst, k):
        def step(i, carry):
            peer = lax.rem(me + i, n_ch)
            pltpu.make_async_remote_copy(
                src_ref=make_src(peer),
                dst_ref=make_dst(),
                send_sem=send.at[k],
                recv_sem=recv.at[k],
                device_id={"lat": lat, "lon": lon, "ch": peer},
                device_id_type=MESH,
            ).start()
            return carry

        lax.fori_loop(1, n_ch, step, 0)

    def fold_start(buffer, gathered, k):
        def step(i, carry):
            fold_copy(buffer, gathered, i, k).start()
            return carry

        lax.fori_loop(1, n_lon, step, 0)

    halo_start(ext, halo_send, halo_recv)

    @pl.when(lat_last)
    def _():
        fold_start(ext, fold_rows, 0)

    own_weights = weights.at[part, me, mine]
    channel_copies(lambda peer: own_weights, lambda: own_weights, 1)

    loads[3].wait()
    masked_cot = (cot_ref[...] * mask_half[None]).reshape(cells, cols)
    cot_rows[...] = dot(to_rows, masked_cot).astype(BF16).reshape(rows, chans, cols)
    channel_copies(lambda peer: cot_rows.at[peer], lambda: cot_all.at[me], 2)
    cot_all[me] = cot_rows[me]

    loads[2].wait()
    for t in range(TAPS * TAPS):
        tap = jnp.broadcast_to(kernel_ref[:, t : t + 1].astype(F32), (chans, EDGE))
        taps[0, t] = tap
        taps[1, TAPS * TAPS - 1 - t] = tap

    loads[4].wait()

    full_width = n_lon * cols
    turn = partner_ref[0]
    first = lax.rem(turn - lon * cols - (cols + HALO - 1) + 2 * full_width, full_width)
    first_block = first // cols
    origin = lax.rem(turn - lon * cols + EDGE - first_block * cols + 3 * full_width, full_width)

    @pl.when(lat_last)
    def _():
        source = lax.broadcasted_iota(jnp.int32, (3 * cols, wide), 0)
        want = origin - lax.broadcasted_iota(jnp.int32, (3 * cols, wide), 1)
        want = jnp.where(want < 0, want + full_width, want)
        pick[...] = (source == want).astype(BF16)

    def fold_fill(buffer, gathered):
        found = jnp.zeros((HALO * chans, wide), F32)
        for j in range(3):
            piece = gathered[lax.rem(first_block + j, n_lon)].reshape(HALO * chans, cols)
            found = found + dot(piece, pick[j * cols : (j + 1) * cols, :])
        found = found.astype(BF16).reshape(HALO, chans, wide)
        for j in range(HALO):
            buffer[HALO + rows + j] = found[HALO - 1 - j]

    def conv(buffer, table, start, stop):
        def step(e, carry):
            line = buffer[e].astype(F32)
            shifted = [
                line[:, EDGE - HALO + b : EDGE - HALO + b + cols] for b in range(TAPS)
            ]
            for a in range(TAPS):
                total = acc[e - a + TAPS - 1]
                for b in range(TAPS):
                    tap = taps[table, a * TAPS + b]
                    total = total + jnp.concatenate([tap] * (cols // EDGE), axis=1) * shifted[b]
                acc[e - a + TAPS - 1] = total
            return carry

        lax.fori_loop(start, stop, step, 0)

    def square_copy(k):
        turn, flip = square[k]
        piece = weights.at[part, :, mine]
        return pltpu.make_async_remote_copy(
            src_ref=piece,
            dst_ref=piece,
            send_sem=square_send.at[k],
            recv_sem=square_recv.at[k],
            device_id=in_square(turn, flip),
            device_id_type=MESH,
        )

    last_rows = HALO + rows
    acc[...] = jnp.zeros(acc.shape, F32)
    halo_arrived(ext, halo_send, halo_recv)
    several(weights.at[part, :, mine], n_ch - 1, 1).wait_recv()
    for k in range(len(square)):
        square_copy(k).start()
    conv(ext, 0, 0, last_rows)

    @pl.when(lat_last)
    def _():
        several(fold_rows, n_lon - 1, 0).wait_recv()
        fold_fill(ext, fold_rows)

    conv(ext, 0, last_rows, last_rows + HALO)
    depth_rows[...] = acc[pl.ds(TAPS - 1, rows)].astype(BF16)
    channel_copies(lambda peer: depth_rows.at[peer], lambda: depth_all.at[me], 3)
    depth_all[me] = depth_rows[me]
    acc[...] = jnp.zeros(acc.shape, F32)

    def swap_weights(half):
        return pltpu.make_async_remote_copy(
            src_ref=weights.at[half],
            dst_ref=weights.at[half],
            send_sem=send.at[4],
            recv_sem=recv.at[4],
            device_id={"lat": sibling, "lon": lon, "ch": me},
            device_id_type=MESH,
        )

    for k in range(len(square)):
        square_copy(k).wait_recv()
    swap_weights(part).start()
    several(cot_all, n_ch - 1, 2).wait_recv()
    several(depth_all, n_ch - 1, 3).wait_recv()

    channels = n_ch * chans
    values = depth_all[...].reshape(channels, cols).astype(F32)
    spread = values - jnp.mean(values, axis=0, keepdims=True)
    inv_scale = lax.rsqrt(jnp.mean(spread * spread, axis=0, keepdims=True) + EPSILON)
    normed_ref[...] = spread * inv_scale
    normed_half = normed_ref[...].astype(BF16)
    cot_here = cot_all[...].reshape(channels, cols)
    swap_weights(1 - part).wait_recv()

    mixed = jnp.zeros((channels, cols), F32)
    back_norm = jnp.zeros((channels, cols), F32)
    per_chunk = n_ch // 4
    for j in range(4):
        span = slice(j * per_chunk, (j + 1) * per_chunk)
        expand = weights[0, span].reshape(per_chunk * hidden_here, channels)
        project = weights[1, span].reshape(per_chunk * hidden_here, channels)
        active, slope = gelu_parts(dot(expand, normed_half))
        back_hidden = (dot(project, cot_here) * slope).astype(BF16)
        mixed = mixed + dot(project, active.astype(BF16), ((0,), (0,)))
        back_norm = back_norm + dot(expand, back_hidden, ((0,), (0,)))
    normed = normed_ref[...]
    mean_plain = jnp.mean(back_norm, axis=0, keepdims=True)
    mean_cross = jnp.mean(back_norm * normed, axis=0, keepdims=True)
    grad_send[...] = (
        (inv_scale * (back_norm - mean_plain - normed * mean_cross))
        .astype(BF16)
        .reshape(n_ch, chans, cols)
    )
    back_row = ext_back.at[HALO + me, :, own_lanes]
    channel_copies(lambda peer: grad_send.at[peer], lambda: back_row, 5)
    ext_back[HALO + me, :, own_lanes] = grad_send[me]
    mixed_send[...] = mixed.astype(BF16).reshape(n_ch, chans, cols)
    channel_copies(lambda peer: mixed_send.at[peer], lambda: mixed_rows.at[me], 6)
    mixed_rows[me] = mixed_send[me]

    several(grad_send, n_ch - 1, 5).wait_recv()
    halo_start(ext_back, halo_send_back, halo_recv_back)

    @pl.when(lat_last)
    def _():
        fold_start(ext_back, fold_rows_back, 7)
        fold_rows_back[lon] = ext_back[pl.ds(rows, HALO), :, own_lanes]

    halo_arrived(ext_back, halo_send_back, halo_recv_back)
    conv(ext_back, 1, 0, last_rows)

    @pl.when(lat_last)
    def _():
        several(fold_rows_back, n_lon - 1, 7).wait_recv()
        fold_fill(ext_back, fold_rows_back)

    conv(ext_back, jnp.where(lat_last, 0, 1), last_rows, last_rows + HALO)
    ocean = mask_ref[...].astype(F32)
    grad_rows[...] = (
        cot_rows[...].astype(F32) + ocean[:, None, :] * acc[pl.ds(TAPS - 1, rows)]
    ).astype(BF16)
    several(mixed_rows, n_ch - 1, 6).wait_recv()

    halo_sent(ext, halo_send, halo_recv)
    halo_sent(ext_back, halo_send_back, halo_recv_back)

    @pl.when(lat_last)
    def _():
        several(fold_rows, n_lon - 1, 0).wait_send()
        several(fold_rows_back, n_lon - 1, 7).wait_send()

    several(weights.at[part, :, mine], n_ch - 1, 1).wait_send()
    for k in range(len(square)):
        square_copy(k).wait_send()
    several(cot_rows, n_ch - 1, 2).wait_send()
    several(depth_rows, n_ch - 1, 3).wait_send()
    swap_weights(part).wait_send()
    several(grad_send, n_ch - 1, 5).wait_send()
    several(mixed_send, n_ch - 1, 6).wait_send()


def finish_kernel(state_ref, mask_ref, mixed_rows, grad_rows, out_ref, grad_ref):
    chans, rows, cols = state_ref.shape
    cells = rows * chans
    swap_row = lax.broadcasted_iota(jnp.int32, (cells, cells), 0)
    swap_col = lax.broadcasted_iota(jnp.int32, (cells, cells), 1)
    to_chans = (swap_col == lax.rem(swap_row, rows) * chans + swap_row // rows).astype(BF16)
    mixed = dot(to_chans, mixed_rows[...].reshape(cells, cols)).reshape(chans, rows, cols)
    ocean = mask_ref[...].astype(F32)
    out_ref[...] = (ocean[None] * (state_ref[...].astype(F32) + mixed)).astype(BF16)
    grad_ref[...] = (
        dot(to_chans, grad_rows[...].reshape(cells, cols))
        .astype(BF16)
        .reshape(chans, rows, cols)
    )


def on_device(state_field, land_mask, partner, kernel, w_expand, w_project, cotangent):
    n_lat, n_lon, n_ch = (lax.axis_size(name) for name in ("lat", "lon", "ch"))
    chans, rows, cols = state_field.shape
    hidden_here = w_project.shape[0]
    assert rows == n_ch and n_lat % 2 == 0
    wide = cols + 2 * EDGE
    channels = n_ch * chans
    sizes = (n_lat, n_lon, n_ch, rows, chans, cols, hidden_here)
    vmem = pl.BlockSpec(memory_space=pltpu.VMEM)
    tile_rows = rows + 2 * HALO
    by_row = jax.ShapeDtypeStruct((rows, chans, cols), BF16)
    mixed_rows, grad_rows = pl.pallas_call(
        functools.partial(block_kernel, sizes),
        out_shape=(by_row, by_row),
        in_specs=[pl.BlockSpec(memory_space=pltpu.HBM)] * 7,
        out_specs=(vmem, vmem),
        scratch_shapes=[
            pltpu.SMEM(partner.shape, jnp.int32),
            pltpu.VMEM(state_field.shape, BF16),
            pltpu.VMEM(land_mask.shape, jnp.int32),
            pltpu.VMEM(kernel.shape, BF16),
            pltpu.VMEM(cotangent.shape, BF16),
            pltpu.VMEM((tile_rows, chans, wide), BF16),
            pltpu.VMEM((tile_rows, chans, wide), BF16),
            pltpu.VMEM((n_lon, HALO, chans, cols), BF16),
            pltpu.VMEM((n_lon, HALO, chans, cols), BF16),
            pltpu.VMEM((3 * cols, wide), BF16),
            pltpu.VMEM((2, TAPS * TAPS, chans, EDGE), F32),
            pltpu.VMEM((rows + 2 * (TAPS - 1), chans, cols), F32),
            pltpu.VMEM((rows, chans, cols), BF16),
            pltpu.VMEM((n_ch, chans, cols), BF16),
            pltpu.VMEM((rows, chans, cols), BF16),
            pltpu.VMEM((n_ch, chans, cols), BF16),
            pltpu.VMEM((2, n_ch, hidden_here, channels), BF16),
            pltpu.VMEM((channels, cols), F32),
            pltpu.VMEM((n_ch, chans, cols), BF16),
            pltpu.VMEM((n_ch, chans, cols), BF16),
            pltpu.SemaphoreType.DMA((8,)),
            pltpu.SemaphoreType.DMA((8,)),
            pltpu.SemaphoreType.DMA((8,)),
            pltpu.SemaphoreType.DMA((8,)),
            pltpu.SemaphoreType.DMA((8,)),
            pltpu.SemaphoreType.DMA((8,)),
            pltpu.SemaphoreType.DMA((n_lat - 1,)),
            pltpu.SemaphoreType.DMA((n_lat - 1,)),
            pltpu.SemaphoreType.DMA((6,)),
        ],
        compiler_params=pltpu.CompilerParams(
            collective_id=0, has_side_effects=True, vmem_limit_bytes=64 * 1000 * 1000
        ),
        name="ocean_block",
    )(partner, state_field, land_mask, kernel, w_expand.T, w_project, cotangent)
    return pl.pallas_call(
        finish_kernel,
        out_shape=(jax.ShapeDtypeStruct(state_field.shape, BF16),) * 2,
        in_specs=[vmem] * 4,
        out_specs=(vmem, vmem),
        name="finish",
    )(state_field, land_mask, mixed_rows, grad_rows)


def solution(mesh):
    placed = (
        P("ch", "lat", "lon"),
        P("lat", "lon"),
        P(),
        P("ch", None),
        P(None, "ch"),
        P("ch", None),
        P("ch", "lat", "lon"),
    )
    return jax.shard_map(
        on_device,
        mesh=mesh,
        in_specs=placed,
        out_specs=(P("ch", "lat", "lon"), P("ch", "lat", "lon")),
        check_vma=False,
    )
```

```python
import functools

import jax
import jax.numpy as jnp
from jax import lax
from jax.experimental import pallas as pl
from jax.experimental.pallas import tpu as pltpu
from jax.sharding import PartitionSpec as P

EPSILON = 1e-06
HALO = 3
EDGE = 128
TAPS = 7
DIRECTIONS = ((-1, 0), (1, 0), (0, -1), (0, 1), (-1, -1), (-1, 1), (1, -1), (1, 1))
MESH = pl.DeviceIdType.MESH
F32 = jnp.float32
BF16 = jnp.bfloat16


def dot(a, b, dims=((1,), (0,))):
    return lax.dot_general(a, b, (dims, ((), ())), preferred_element_type=F32)


def gelu_parts(hidden):
    normal_cdf = 0.5 * (1.0 + lax.erf(hidden * 0.7071067811865476))
    return (
        hidden * normal_cdf,
        normal_cdf + hidden * jnp.exp(-0.5 * hidden * hidden) * 0.3989422804014327,
    )


def block_kernel(
    sizes,
    partner_hbm,
    state_hbm,
    mask_hbm,
    kernel_hbm,
    expand_hbm,
    project_hbm,
    cot_hbm,
    state_sum,
    grad_sum,
    partner_ref,
    state_ref,
    mask_ref,
    kernel_ref,
    cot_ref,
    ext,
    ext_back,
    fold_rows,
    fold_rows_back,
    pick,
    taps,
    acc,
    edge_taps,
    edge_acc,
    cot_rows,
    cot_all,
    depth_rows,
    depth_all,
    weights,
    weights_send,
    normed_ref,
    mixed_send,
    grad_send,
    mixed_rows,
    halo_send,
    halo_recv,
    halo_send_back,
    halo_recv_back,
    send,
    recv,
    square_send,
    square_recv,
    load,
):
    n_lat, n_lon, n_ch, rows, chans, cols, hidden_here = sizes
    wide = cols + 2 * EDGE
    cells = rows * chans
    lat, lon, me = lax.axis_index("lat"), lax.axis_index("lon"), lax.axis_index("ch")
    lat_last = lat == n_lat - 1
    part = lax.rem(lat, 2)
    sibling = lat + 1 - 2 * part
    pairs = n_lat // 2
    share = hidden_here // (2 * pairs)
    across = lax.rem(lat + pairs, n_lat)

    def share_of(row_block):
        index = row_block // 2 * 2 + lax.rem(lon, 2)
        return pl.ds(pl.multiple_of(index * share, share), share)

    mine, given = share_of(across), share_of(lat)
    lon_twin = lon + 1 - 2 * lax.rem(lon, 2)
    square = [(0, 1)] + [(2 * i, j) for i in range(1, pairs) for j in (0, 1)]

    def in_square(turn, flip):
        return {
            "lat": lax.rem(lat + turn, n_lat),
            "lon": lon_twin if flip else lon,
            "ch": me,
        }
    own_rows = pl.ds(HALO, rows)
    own_lanes = pl.ds(EDGE, cols)

    def exists(dl):
        return jnp.logical_and(lat + dl >= 0, lat + dl < n_lat)

    def at(dl, do):
        return {"lat": lat + dl, "lon": lax.rem(lon + do + n_lon, n_lon), "ch": me}

    barrier = pltpu.get_barrier_semaphore()

    def greet_channel(i, carry):
        pl.semaphore_signal(
            barrier,
            device_id={"lat": across, "lon": lon, "ch": i},
            device_id_type=MESH,
        )
        return carry

    def greet_fold(i, carry):
        pl.semaphore_signal(
            barrier,
            device_id={"lat": lat, "lon": lax.rem(lon + i, n_lon), "ch": me},
            device_id_type=MESH,
        )
        return carry

    for dl, do in DIRECTIONS:

        @pl.when(exists(dl))
        def _():
            pl.semaphore_signal(barrier, device_id=at(dl, do), device_id_type=MESH)

    lax.fori_loop(0, n_ch, greet_channel, 0)
    for turn, flip in square[1:]:
        if (turn, flip) == (pairs, 0):
            continue
        pl.semaphore_signal(barrier, device_id=in_square(turn, flip), device_id_type=MESH)

    @pl.when(lat_last)
    def _():
        lax.fori_loop(1, n_lon, greet_fold, 0)

    def fetch(k, src, dst):
        return pltpu.make_async_copy(src, dst, load.at[k])

    loads = [
        fetch(0, state_hbm, state_ref),
        fetch(1, mask_hbm, mask_ref),
        fetch(2, kernel_hbm, kernel_ref),
        fetch(3, cot_hbm, cot_ref),
        fetch(4, partner_hbm, partner_ref),
    ]
    own_expand = [
        fetch(5, expand_hbm.at[mine], weights.at[0, me, mine]),
        fetch(6, expand_hbm.at[given], weights_send),
    ]
    own_project = [
        fetch(5, project_hbm.at[mine], weights.at[1, me, mine]),
        fetch(6, project_hbm.at[given], weights_send),
    ]
    for copy in loads:
        copy.start()

    @pl.when(part == 0)
    def _():
        for copy in own_expand:
            copy.start()

    @pl.when(part == 1)
    def _():
        for copy in own_project:
            copy.start()

    swap_row = lax.broadcasted_iota(jnp.int32, (cells, cells), 0)
    swap_col = lax.broadcasted_iota(jnp.int32, (cells, cells), 1)
    to_rows = (swap_col == lax.rem(swap_row, chans) * rows + swap_row // chans).astype(BF16)
    loads[0].wait()
    loads[1].wait()
    mask_half = mask_ref[...].astype(BF16)
    masked = (state_ref[...] * mask_half[None]).reshape(cells, cols)
    ext[own_rows, :, own_lanes] = (
        dot(to_rows, masked).astype(BF16).reshape(rows, chans, cols)
    )
    @pl.when(lat == 0)
    def _():
        ext[0:HALO] = jnp.zeros((HALO, chans, wide), BF16)
        ext_back[0:HALO] = jnp.zeros((HALO, chans, wide), BF16)

    @pl.when(lat_last)
    def _():
        fold_rows[lon] = ext[pl.ds(rows, HALO), :, own_lanes]

    for copy in own_expand:
        copy.wait()
    neighbours = sum(
        (exists(dl).astype(jnp.int32) for dl, _ in DIRECTIONS), jnp.int32(n_ch + len(square) - 2)
    ) + jnp.where(lat_last, n_lon - 1, 0)
    pl.semaphore_wait(barrier, neighbours)

    def halo_copy(buffer, d, send_sems, recv_sems):
        dl, do = DIRECTIONS[d]
        src_rows, dst_rows = {
            -1: (pl.ds(HALO, HALO), pl.ds(HALO + rows, HALO)),
            0: (own_rows, own_rows),
            1: (pl.ds(rows, HALO), pl.ds(0, HALO)),
        }[dl]
        src_lanes, dst_lanes = {
            -1: (pl.ds(EDGE, EDGE), pl.ds(EDGE + cols, EDGE)),
            0: (own_lanes, own_lanes),
            1: (pl.ds(cols, EDGE), pl.ds(0, EDGE)),
        }[do]
        return pltpu.make_async_remote_copy(
            src_ref=buffer.at[src_rows, :, src_lanes],
            dst_ref=buffer.at[dst_rows, :, dst_lanes],
            send_sem=send_sems.at[d],
            recv_sem=recv_sems.at[d],
            device_id=at(dl, do),
            device_id_type=MESH,
        )

    def halo_start(buffer, send_sems, recv_sems):
        for d, (dl, _) in enumerate(DIRECTIONS):
            pl.when(exists(dl))(lambda d=d: halo_copy(buffer, d, send_sems, recv_sems).start())

    def halo_arrived(buffer, send_sems, recv_sems):
        for d, (dl, _) in enumerate(DIRECTIONS):
            pl.when(exists(-dl))(
                lambda d=d: halo_copy(buffer, d, send_sems, recv_sems).wait_recv()
            )

    def halo_sent(buffer, send_sems, recv_sems):
        for d, (dl, _) in enumerate(DIRECTIONS):
            pl.when(exists(dl))(
                lambda d=d: halo_copy(buffer, d, send_sems, recv_sems).wait_send()
            )

    def fold_copy(buffer, gathered, i, k):
        return pltpu.make_async_remote_copy(
            src_ref=buffer.at[pl.ds(rows, HALO), :, own_lanes],
            dst_ref=gathered.at[lon],
            send_sem=send.at[k],
            recv_sem=recv.at[k],
            device_id={"lat": lat, "lon": lax.rem(lon + i, n_lon), "ch": me},
            device_id_type=MESH,
        )

    def several(gathered, count, k):
        whole = gathered.at[pl.ds(0, count)]
        return pltpu.make_async_remote_copy(
            src_ref=whole,
            dst_ref=whole,
            send_sem=send.at[k],
            recv_sem=recv.at[k],
            device_id={"lat": across, "lon": lon, "ch": me},
            device_id_type=MESH,
        )

    def channel_copies(make_src, dst, k, wanted=None):
        def step(j, carry):
            away = (j + 1) // 2
            peer = lax.rem(me + n_ch // 2 + n_ch + away * (1 - 2 * lax.rem(j, 2)), n_ch)

            def go():
                pltpu.make_async_remote_copy(
                    src_ref=make_src(peer),
                    dst_ref=dst,
                    send_sem=send.at[k],
                    recv_sem=recv.at[k],
                    device_id={"lat": across, "lon": lon, "ch": peer},
                    device_id_type=MESH,
                ).start()

            if wanted is None:
                go()
            else:
                pl.when(wanted(peer))(go)
            return carry

        lax.fori_loop(0, n_ch, step, 0)

    def fold_start(buffer, gathered, k):
        def step(i, carry):
            fold_copy(buffer, gathered, i, k).start()
            return carry

        lax.fori_loop(1, n_lon, step, 0)

    halo_start(ext, halo_send, halo_recv)

    @pl.when(lat_last)
    def _():
        fold_start(ext, fold_rows, 0)

    channel_copies(
        lambda peer: weights_send, weights.at[part, me, given], 1, lambda peer: peer != me
    )
    loads[2].wait()
    for t in range(TAPS * TAPS):
        tap = jnp.broadcast_to(kernel_ref[:, t : t + 1].astype(F32), (chans, EDGE))
        taps[0, t] = tap
        taps[1, TAPS * TAPS - 1 - t] = tap
    lane = lax.broadcasted_iota(jnp.int32, (chans, EDGE), 1)
    for table in range(2):
        for a in range(TAPS):
            for b in range(HALO):
                edge_taps[table, a * HALO + b] = jnp.where(
                    lane < EDGE // 2,
                    taps[table, a * TAPS + b],
                    taps[table, a * TAPS + b + HALO + 1],
                )

    def add_line(line, table, e, a):
        parts = [
            jnp.concatenate([taps[table, a * TAPS + b]] * (cols // EDGE), axis=1)
            * line[:, EDGE - HALO + b : EDGE - HALO + b + cols]
            for b in range(TAPS)
        ]
        acc[e - a + TAPS - 1] += ((parts[0] + parts[1]) + (parts[2] + parts[3])) + (
            (parts[4] + parts[5]) + parts[6]
        )

    def conv_own(buffer, table):
        acc[...] = jnp.zeros(acc.shape, F32)
        edge_acc[...] = jnp.zeros(edge_acc.shape, F32)
        blank = jnp.zeros((chans, EDGE), F32)

        def step(e, carry):
            own = buffer[e, :, own_lanes].astype(F32)
            line = jnp.concatenate([blank, own, blank], axis=1)
            for a in range(TAPS):
                add_line(line, table, e, a)
            return carry

        lax.fori_loop(HALO, HALO + rows, step, 0, unroll=2)

    def conv_edges(buffer, table):
        def step(e, carry):
            left = jnp.where(lane >= EDGE // 2, buffer[e, :, pl.ds(0, EDGE)].astype(F32), 0.0)
            right = jnp.where(
                lane < EDGE // 2, buffer[e, :, pl.ds(EDGE + cols, EDGE)].astype(F32), 0.0
            )
            moved = [
                jnp.where(
                    lane < EDGE // 2,
                    pltpu.roll(left, HALO - b, 1),
                    pltpu.roll(right, EDGE - 1 - b, 1),
                )
                for b in range(HALO)
            ]
            for a in range(TAPS):
                parts = [edge_taps[table, a * HALO + b] * moved[b] for b in range(HALO)]
                edge_acc[e - a + TAPS - 1] += (parts[0] + parts[1]) + parts[2]
            return carry

        lax.fori_loop(HALO, HALO + rows, step, 0, unroll=2)

    def conv_outer(buffer, table, lines):
        for e in lines:
            line = buffer[e].astype(F32)
            for a in range(TAPS):
                if 0 <= e - a < rows:
                    add_line(line, table, e, a)

    def conv_total(start, count):
        edge = edge_acc[pl.ds(TAPS - 1 + start, count)]
        both = jnp.concatenate(
            [
                jnp.where(lane < EDGE // 2, edge, 0.0),
                jnp.zeros((count, chans, cols - 2 * EDGE), F32),
                jnp.where(lane < EDGE // 2, 0.0, edge),
            ][:: 1 if cols > 2 * EDGE else 2],
            axis=2,
        )
        return acc[pl.ds(TAPS - 1 + start, count)] + both

    below, above = range(HALO), range(HALO + rows, HALO + rows + HALO)
    settled = rows - HALO

    conv_own(ext, 0)

    loads[3].wait()
    masked_cot = (cot_ref[...] * mask_half[None]).reshape(cells, cols)
    cot_rows[...] = dot(to_rows, masked_cot).astype(BF16).reshape(rows, chans, cols)
    channel_copies(lambda peer: cot_rows.at[peer], cot_all.at[me], 2)

    loads[4].wait()

    full_width = n_lon * cols
    turn = partner_ref[0]
    first = lax.rem(turn - lon * cols - (cols + HALO - 1) + 2 * full_width, full_width)
    first_block = first // cols
    origin = lax.rem(turn - lon * cols + EDGE - first_block * cols + 3 * full_width, full_width)

    @pl.when(lat_last)
    def _():
        source = lax.broadcasted_iota(jnp.int32, (3 * cols, wide), 0)
        want = origin - lax.broadcasted_iota(jnp.int32, (3 * cols, wide), 1)
        want = jnp.where(want < 0, want + full_width, want)
        pick[...] = (source == want).astype(BF16)

    def fold_fill(buffer, gathered):
        found = jnp.zeros((HALO * chans, wide), F32)
        for j in range(3):
            piece = gathered[lax.rem(first_block + j, n_lon)].reshape(HALO * chans, cols)
            found = found + dot(piece, pick[j * cols : (j + 1) * cols, :])
        found = found.astype(BF16).reshape(HALO, chans, wide)
        for j in range(HALO):
            buffer[HALO + rows + j] = found[HALO - 1 - j]

    def square_copy(k):
        turn, flip = square[k]
        piece = weights.at[part, :, mine]
        return pltpu.make_async_remote_copy(
            src_ref=piece,
            dst_ref=piece,
            send_sem=square_send.at[k],
            recv_sem=square_recv.at[k],
            device_id=in_square(turn, flip),
            device_id_type=MESH,
        )

    several(weights.at[part, :, mine], n_ch - 1, 1).wait_recv()
    for k in range(len(square)):
        square_copy(k).start()
    halo_arrived(ext, halo_send, halo_recv)
    conv_edges(ext, 0)
    conv_outer(ext, 0, below)
    depth_rows[pl.ds(0, settled)] = conv_total(0, settled).astype(BF16)
    channel_copies(
        lambda peer: depth_rows.at[peer], depth_all.at[me], 3, lambda peer: peer < settled
    )

    @pl.when(lat_last)
    def _():
        several(fold_rows, n_lon - 1, 0).wait_recv()
        fold_fill(ext, fold_rows)

    conv_outer(ext, 0, above)
    depth_rows[pl.ds(settled, HALO)] = conv_total(settled, HALO).astype(BF16)
    channel_copies(
        lambda peer: depth_rows.at[peer], depth_all.at[me], 3, lambda peer: peer >= settled
    )

    def swap_weights(half):
        return pltpu.make_async_remote_copy(
            src_ref=weights.at[half],
            dst_ref=weights.at[half],
            send_sem=send.at[4],
            recv_sem=recv.at[4],
            device_id={"lat": sibling, "lon": lon, "ch": me},
            device_id_type=MESH,
        )

    for k in range(len(square)):
        square_copy(k).wait_recv()
    swap_weights(part).start()
    several(cot_all, n_ch, 2).wait_recv()
    several(depth_all, n_ch, 3).wait_recv()

    channels = n_ch * chans
    values = depth_all[...].reshape(channels, cols).astype(F32)
    spread = values - jnp.mean(values, axis=0, keepdims=True)
    inv_scale = lax.rsqrt(jnp.mean(spread * spread, axis=0, keepdims=True) + EPSILON)
    normed_ref[...] = spread * inv_scale
    normed_half = normed_ref[...].astype(BF16)
    cot_here = cot_all[...].reshape(channels, cols)
    swap_weights(1 - part).wait_recv()

    mixed = jnp.zeros((channels, cols), F32)
    back_norm = jnp.zeros((channels, cols), F32)
    per_chunk = n_ch // 4
    for j in range(4):
        span = slice(j * per_chunk, (j + 1) * per_chunk)
        expand = weights[0, span].reshape(per_chunk * hidden_here, channels)
        project = weights[1, span].reshape(per_chunk * hidden_here, channels)
        active, slope = gelu_parts(dot(expand, normed_half))
        back_hidden = (dot(project, cot_here) * slope).astype(BF16)
        mixed = mixed + dot(project, active.astype(BF16), ((0,), (0,)))
        back_norm = back_norm + dot(expand, back_hidden, ((0,), (0,)))
    normed = normed_ref[...]
    mean_plain = jnp.mean(back_norm, axis=0, keepdims=True)
    mean_cross = jnp.mean(back_norm * normed, axis=0, keepdims=True)
    grad_send[...] = (
        (inv_scale * (back_norm - mean_plain - normed * mean_cross))
        .astype(BF16)
        .reshape(n_ch, chans, cols)
    )
    channel_copies(lambda peer: grad_send.at[peer], ext_back.at[HALO + me, :, own_lanes], 5)
    mixed_send[...] = mixed.astype(BF16).reshape(n_ch, chans, cols)
    channel_copies(lambda peer: mixed_send.at[peer], mixed_rows.at[me], 6)

    several(grad_send, n_ch, 5).wait_recv()
    halo_start(ext_back, halo_send_back, halo_recv_back)

    @pl.when(lat_last)
    def _():
        fold_start(ext_back, fold_rows_back, 7)
        fold_rows_back[lon] = ext_back[pl.ds(rows, HALO), :, own_lanes]

    conv_own(ext_back, 1)
    to_chans = (swap_col == lax.rem(swap_row, rows) * chans + swap_row // rows).astype(BF16)
    several(mixed_rows, n_ch, 6).wait_recv()
    mixed_here = dot(to_chans, mixed_rows[...].reshape(cells, cols)).reshape(chans, rows, cols)
    state_sum[...] = (state_ref[...].astype(F32) + mixed_here).astype(BF16)

    halo_arrived(ext_back, halo_send_back, halo_recv_back)
    conv_edges(ext_back, 1)
    conv_outer(ext_back, 1, below)

    @pl.when(lat_last)
    def _():
        several(fold_rows_back, n_lon - 1, 7).wait_recv()
        fold_fill(ext_back, fold_rows_back)

    conv_outer(ext_back, jnp.where(lat_last, 0, 1), above)
    ocean = mask_ref[...].astype(F32)
    grad_rows = (
        cot_rows[...].astype(F32) + ocean[:, None, :] * conv_total(0, rows)
    ).astype(BF16)
    grad_sum[...] = (
        dot(to_chans, grad_rows.reshape(cells, cols)).astype(BF16).reshape(chans, rows, cols)
    )

    halo_sent(ext, halo_send, halo_recv)
    halo_sent(ext_back, halo_send_back, halo_recv_back)

    @pl.when(lat_last)
    def _():
        several(fold_rows, n_lon - 1, 0).wait_send()
        several(fold_rows_back, n_lon - 1, 7).wait_send()

    several(weights.at[part, :, mine], n_ch - 1, 1).wait_send()
    for k in range(len(square)):
        square_copy(k).wait_send()
    several(cot_rows, n_ch, 2).wait_send()
    several(depth_rows, n_ch, 3).wait_send()
    swap_weights(part).wait_send()
    several(grad_send, n_ch, 5).wait_send()
    several(mixed_send, n_ch, 6).wait_send()


def on_device(state_field, land_mask, partner, kernel, w_expand, w_project, cotangent):
    n_lat, n_lon, n_ch = (lax.axis_size(name) for name in ("lat", "lon", "ch"))
    chans, rows, cols = state_field.shape
    hidden_here = w_project.shape[0]
    assert rows == n_ch and n_lat % 2 == 0
    wide = cols + 2 * EDGE
    channels = n_ch * chans
    sizes = (n_lat, n_lon, n_ch, rows, chans, cols, hidden_here)
    vmem = pl.BlockSpec(memory_space=pltpu.VMEM)
    tile_rows = rows + 2 * HALO
    state_sum, grad_sum = pl.pallas_call(
        functools.partial(block_kernel, sizes),
        out_shape=(jax.ShapeDtypeStruct(state_field.shape, BF16),) * 2,
        in_specs=[pl.BlockSpec(memory_space=pltpu.HBM)] * 7,
        out_specs=(vmem, vmem),
        scratch_shapes=[
            pltpu.SMEM(partner.shape, jnp.int32),
            pltpu.VMEM(state_field.shape, BF16),
            pltpu.VMEM(land_mask.shape, jnp.int32),
            pltpu.VMEM(kernel.shape, BF16),
            pltpu.VMEM(cotangent.shape, BF16),
            pltpu.VMEM((tile_rows, chans, wide), BF16),
            pltpu.VMEM((tile_rows, chans, wide), BF16),
            pltpu.VMEM((n_lon, HALO, chans, cols), BF16),
            pltpu.VMEM((n_lon, HALO, chans, cols), BF16),
            pltpu.VMEM((3 * cols, wide), BF16),
            pltpu.VMEM((2, TAPS * TAPS, chans, EDGE), F32),
            pltpu.VMEM((rows + 2 * (TAPS - 1), chans, cols), F32),
            pltpu.VMEM((2, TAPS * HALO, chans, EDGE), F32),
            pltpu.VMEM((rows + 2 * (TAPS - 1), chans, EDGE), F32),
            pltpu.VMEM((rows, chans, cols), BF16),
            pltpu.VMEM((n_ch, chans, cols), BF16),
            pltpu.VMEM((rows, chans, cols), BF16),
            pltpu.VMEM((n_ch, chans, cols), BF16),
            pltpu.VMEM((2, n_ch, hidden_here, channels), BF16),
            pltpu.VMEM((hidden_here // n_lat, channels), BF16),
            pltpu.VMEM((channels, cols), F32),
            pltpu.VMEM((n_ch, chans, cols), BF16),
            pltpu.VMEM((n_ch, chans, cols), BF16),
            pltpu.VMEM((n_ch, chans, cols), BF16),
            pltpu.SemaphoreType.DMA((8,)),
            pltpu.SemaphoreType.DMA((8,)),
            pltpu.SemaphoreType.DMA((8,)),
            pltpu.SemaphoreType.DMA((8,)),
            pltpu.SemaphoreType.DMA((8,)),
            pltpu.SemaphoreType.DMA((8,)),
            pltpu.SemaphoreType.DMA((n_lat - 1,)),
            pltpu.SemaphoreType.DMA((n_lat - 1,)),
            pltpu.SemaphoreType.DMA((7,)),
        ],
        compiler_params=pltpu.CompilerParams(
            collective_id=0, has_side_effects=True, vmem_limit_bytes=64 * 1000 * 1000
        ),
        name="ocean_block",
    )(partner, state_field, land_mask, kernel, w_expand.T, w_project, cotangent)
    mask_half = land_mask.astype(BF16)[None]
    return (state_sum * mask_half, grad_sum * mask_half)


def solution(mesh):
    placed = (
        P("ch", "lat", "lon"),
        P("lat", "lon"),
        P(),
        P("ch", None),
        P(None, "ch"),
        P("ch", None),
        P("ch", "lat", "lon"),
    )
    return jax.shard_map(
        on_device,
        mesh=mesh,
        in_specs=placed,
        out_specs=(P("ch", "lat", "lon"), P("ch", "lat", "lon")),
        check_vma=False,
    )
```

```python
import functools

import jax
import jax.numpy as jnp
from jax import lax
from jax.experimental import pallas as pl
from jax.experimental.pallas import tpu as pltpu
from jax.sharding import PartitionSpec as P

EPSILON = 1e-06
HALO = 3
EDGE = 128
TAPS = 7
DIRECTIONS = ((-1, 0), (1, 0), (0, -1), (0, 1), (-1, -1), (-1, 1), (1, -1), (1, 1))
MESH = pl.DeviceIdType.MESH
F32 = jnp.float32
BF16 = jnp.bfloat16


def dot(a, b, dims=((1,), (0,))):
    return lax.dot_general(a, b, (dims, ((), ())), preferred_element_type=F32)


def gelu_parts(hidden):
    normal_cdf = 0.5 * (1.0 + lax.erf(hidden * 0.7071067811865476))
    return (
        hidden * normal_cdf,
        normal_cdf + hidden * jnp.exp(-0.5 * hidden * hidden) * 0.3989422804014327,
    )


def block_kernel(
    sizes,
    partner_hbm,
    state_hbm,
    mask_hbm,
    kernel_hbm,
    expand_hbm,
    project_hbm,
    cot_hbm,
    state_sum,
    grad_sum,
    partner_ref,
    state_ref,
    mask_ref,
    kernel_ref,
    cot_ref,
    ext,
    ext_back,
    fold_rows,
    fold_rows_back,
    pick,
    taps,
    acc,
    edge_taps,
    edge_acc,
    edge_out,
    edge_in,
    edge_tile,
    cot_rows,
    cot_all,
    depth_rows,
    depth_all,
    weights,
    weights_send,
    normed_ref,
    mixed_send,
    grad_send,
    mixed_rows,
    halo_send,
    halo_recv,
    halo_send_back,
    halo_recv_back,
    send,
    recv,
    square_send,
    square_recv,
    load,
):
    n_lat, n_lon, n_ch, rows, chans, cols, hidden_here = sizes
    wide = cols + 2 * EDGE
    cells = rows * chans
    lat, lon, me = lax.axis_index("lat"), lax.axis_index("lon"), lax.axis_index("ch")
    lat_last = lat == n_lat - 1
    part = lax.rem(lat, 2)
    sibling = lat + 1 - 2 * part
    pairs = n_lat // 2
    share = hidden_here // (2 * pairs)
    across = lax.rem(lat + pairs, n_lat)

    def share_of(row_block):
        index = row_block // 2 * 2 + lax.rem(lon, 2)
        return pl.ds(pl.multiple_of(index * share, share), share)

    mine, given = share_of(across), share_of(lat)
    lon_twin = lon + 1 - 2 * lax.rem(lon, 2)
    square = [(0, 1)] + [(2 * i, j) for i in range(1, pairs) for j in (0, 1)]

    def in_square(turn, flip):
        return {
            "lat": lax.rem(lat + turn, n_lat),
            "lon": lon_twin if flip else lon,
            "ch": me,
        }
    own_rows = pl.ds(HALO, rows)
    own_lanes = pl.ds(EDGE, cols)

    def exists(dl):
        return jnp.logical_and(lat + dl >= 0, lat + dl < n_lat)

    def at(dl, do):
        return {"lat": lat + dl, "lon": lax.rem(lon + do + n_lon, n_lon), "ch": me}

    barrier = pltpu.get_barrier_semaphore()

    def greet_channel(i, carry):
        pl.semaphore_signal(
            barrier,
            device_id={"lat": across, "lon": lon, "ch": i},
            device_id_type=MESH,
        )
        return carry

    def greet_fold(i, carry):
        pl.semaphore_signal(
            barrier,
            device_id={"lat": lat, "lon": lax.rem(lon + i, n_lon), "ch": me},
            device_id_type=MESH,
        )
        return carry

    for dl, do in DIRECTIONS:

        @pl.when(exists(dl))
        def _():
            pl.semaphore_signal(barrier, device_id=at(dl, do), device_id_type=MESH)

    lax.fori_loop(0, n_ch, greet_channel, 0)
    for turn, flip in square[1:]:
        if (turn, flip) == (pairs, 0):
            continue
        pl.semaphore_signal(barrier, device_id=in_square(turn, flip), device_id_type=MESH)

    @pl.when(lat_last)
    def _():
        lax.fori_loop(1, n_lon, greet_fold, 0)

    def fetch(k, src, dst):
        return pltpu.make_async_copy(src, dst, load.at[k])

    loads = [
        fetch(0, state_hbm, state_ref),
        fetch(1, mask_hbm, mask_ref),
        fetch(2, kernel_hbm, kernel_ref),
        fetch(3, cot_hbm, cot_ref),
        fetch(4, partner_hbm, partner_ref),
    ]
    own_expand = [
        fetch(5, expand_hbm.at[mine], weights.at[0, me, mine]),
        fetch(6, expand_hbm.at[given], weights_send),
    ]
    own_project = [
        fetch(5, project_hbm.at[mine], weights.at[1, me, mine]),
        fetch(6, project_hbm.at[given], weights_send),
    ]
    for copy in loads:
        copy.start()

    @pl.when(part == 0)
    def _():
        for copy in own_expand:
            copy.start()

    @pl.when(part == 1)
    def _():
        for copy in own_project:
            copy.start()

    swap_row = lax.broadcasted_iota(jnp.int32, (cells, cells), 0)
    swap_col = lax.broadcasted_iota(jnp.int32, (cells, cells), 1)
    to_rows = (swap_col == lax.rem(swap_row, chans) * rows + swap_row // chans).astype(BF16)
    loads[0].wait()
    loads[1].wait()
    mask_half = mask_ref[...].astype(BF16)
    masked = (state_ref[...] * mask_half[None]).reshape(cells, cols)
    own_cells = dot(to_rows, masked).astype(BF16)
    ext[own_rows, :, own_lanes] = own_cells.reshape(rows, chans, cols)

    slot = lax.broadcasted_iota(jnp.int32, (2 * 8, EDGE), 0)
    spot = lax.broadcasted_iota(jnp.int32, (2 * 8, EDGE), 1)
    first_cols = jnp.logical_and(slot < HALO, spot == slot).astype(BF16)
    last_cols = jnp.logical_and(slot < HALO, spot == slot + EDGE - HALO).astype(BF16)

    def pack_edges(block, phase):
        edge_out[phase, 0] = dot(first_cols, block[:, :EDGE], ((1,), (1,))).astype(BF16)
        edge_out[phase, 1] = dot(last_cols, block[:, cols - EDGE :], ((1,), (1,))).astype(BF16)

    def unpack_edges(phase):
        both = dot(edge_in[phase, 0], last_cols, ((0,), (0,))) + dot(
            edge_in[phase, 1], first_cols, ((0,), (0,))
        )
        edge_tile[...] = both.reshape(rows, chans, EDGE)

    pack_edges(own_cells, 0)
    @pl.when(lat == 0)
    def _():
        ext[0:HALO] = jnp.zeros((HALO, chans, wide), BF16)
        ext_back[0:HALO] = jnp.zeros((HALO, chans, wide), BF16)

    @pl.when(lat_last)
    def _():
        fold_rows[lon] = ext[pl.ds(rows, HALO), :, own_lanes]

    for copy in own_expand:
        copy.wait()
    neighbours = sum(
        (exists(dl).astype(jnp.int32) for dl, _ in DIRECTIONS), jnp.int32(n_ch + len(square) - 2)
    ) + jnp.where(lat_last, n_lon - 1, 0)
    pl.semaphore_wait(barrier, neighbours)

    def halo_copy(buffer, d, send_sems, recv_sems):
        dl, do = DIRECTIONS[d]
        if dl == 0:
            phase = 0 if buffer is ext else 1
            return pltpu.make_async_remote_copy(
                src_ref=edge_out.at[phase, (1 + do) // 2],
                dst_ref=edge_in.at[phase, (1 - do) // 2],
                send_sem=send_sems.at[d],
                recv_sem=recv_sems.at[d],
                device_id=at(dl, do),
                device_id_type=MESH,
            )
        src_rows, dst_rows = {
            -1: (pl.ds(HALO, HALO), pl.ds(HALO + rows, HALO)),
            1: (pl.ds(rows, HALO), pl.ds(0, HALO)),
        }[dl]
        src_lanes, dst_lanes = {
            -1: (pl.ds(EDGE, EDGE), pl.ds(EDGE + cols, EDGE)),
            0: (own_lanes, own_lanes),
            1: (pl.ds(cols, EDGE), pl.ds(0, EDGE)),
        }[do]
        return pltpu.make_async_remote_copy(
            src_ref=buffer.at[src_rows, :, src_lanes],
            dst_ref=buffer.at[dst_rows, :, dst_lanes],
            send_sem=send_sems.at[d],
            recv_sem=recv_sems.at[d],
            device_id=at(dl, do),
            device_id_type=MESH,
        )

    def halo_start(buffer, send_sems, recv_sems):
        for d, (dl, _) in enumerate(DIRECTIONS):
            pl.when(exists(dl))(lambda d=d: halo_copy(buffer, d, send_sems, recv_sems).start())

    def halo_arrived(buffer, send_sems, recv_sems):
        for d, (dl, _) in enumerate(DIRECTIONS):
            pl.when(exists(-dl))(
                lambda d=d: halo_copy(buffer, d, send_sems, recv_sems).wait_recv()
            )

    def halo_sent(buffer, send_sems, recv_sems):
        for d, (dl, _) in enumerate(DIRECTIONS):
            pl.when(exists(dl))(
                lambda d=d: halo_copy(buffer, d, send_sems, recv_sems).wait_send()
            )

    def fold_copy(buffer, gathered, i, k):
        return pltpu.make_async_remote_copy(
            src_ref=buffer.at[pl.ds(rows, HALO), :, own_lanes],
            dst_ref=gathered.at[lon],
            send_sem=send.at[k],
            recv_sem=recv.at[k],
            device_id={"lat": lat, "lon": lax.rem(lon + i, n_lon), "ch": me},
            device_id_type=MESH,
        )

    def several(gathered, count, k):
        whole = gathered.at[pl.ds(0, count)]
        return pltpu.make_async_remote_copy(
            src_ref=whole,
            dst_ref=whole,
            send_sem=send.at[k],
            recv_sem=recv.at[k],
            device_id={"lat": across, "lon": lon, "ch": me},
            device_id_type=MESH,
        )

    def channel_copies(make_src, dst, k, wanted=None):
        def step(j, carry):
            away = (j + 1) // 2
            peer = lax.rem(me + n_ch // 2 + n_ch + away * (1 - 2 * lax.rem(j, 2)), n_ch)

            def go():
                pltpu.make_async_remote_copy(
                    src_ref=make_src(peer),
                    dst_ref=dst,
                    send_sem=send.at[k],
                    recv_sem=recv.at[k],
                    device_id={"lat": across, "lon": lon, "ch": peer},
                    device_id_type=MESH,
                ).start()

            if wanted is None:
                go()
            else:
                pl.when(wanted(peer))(go)
            return carry

        lax.fori_loop(0, n_ch, step, 0)

    def fold_start(buffer, gathered, k):
        def step(j, carry):
            away = (j + 1) // 2
            i = n_lon // 2 + away * (1 - 2 * lax.rem(j, 2))
            fold_copy(buffer, gathered, i, k).start()
            return carry

        lax.fori_loop(0, n_lon - 1, step, 0)

    halo_start(ext, halo_send, halo_recv)

    @pl.when(lat_last)
    def _():
        fold_start(ext, fold_rows, 0)

    channel_copies(
        lambda peer: weights_send, weights.at[part, me, given], 1, lambda peer: peer != me
    )
    loads[2].wait()
    for t in range(TAPS * TAPS):
        tap = jnp.broadcast_to(kernel_ref[:, t : t + 1].astype(F32), (chans, EDGE))
        taps[0, t] = tap
        taps[1, TAPS * TAPS - 1 - t] = tap
    lane = lax.broadcasted_iota(jnp.int32, (chans, EDGE), 1)
    for table in range(2):
        for a in range(TAPS):
            for b in range(HALO):
                edge_taps[table, a * HALO + b] = jnp.where(
                    lane < EDGE // 2,
                    taps[table, a * TAPS + b],
                    taps[table, a * TAPS + b + HALO + 1],
                )

    def add_line(line, table, e, a):
        parts = [
            jnp.concatenate([taps[table, a * TAPS + b]] * (cols // EDGE), axis=1)
            * line[:, EDGE - HALO + b : EDGE - HALO + b + cols]
            for b in range(TAPS)
        ]
        acc[e - a + TAPS - 1] += ((parts[0] + parts[1]) + (parts[2] + parts[3])) + (
            (parts[4] + parts[5]) + parts[6]
        )

    def conv_own(buffer, table):
        acc[...] = jnp.zeros(acc.shape, F32)
        edge_acc[...] = jnp.zeros(edge_acc.shape, F32)
        blank = jnp.zeros((chans, EDGE), F32)

        def step(e, carry):
            own = buffer[e, :, own_lanes].astype(F32)
            line = jnp.concatenate([blank, own, blank], axis=1)
            for a in range(TAPS):
                add_line(line, table, e, a)
            return carry

        lax.fori_loop(HALO, HALO + rows, step, 0, unroll=2)

    def conv_edges(table):
        def step(e, carry):
            tile = edge_tile[e - HALO]
            left = jnp.where(lane >= EDGE // 2, tile, 0.0)
            right = jnp.where(lane < EDGE // 2, tile, 0.0)
            moved = [
                jnp.where(
                    lane < EDGE // 2,
                    pltpu.roll(left, HALO - b, 1),
                    pltpu.roll(right, EDGE - 1 - b, 1),
                )
                for b in range(HALO)
            ]
            for a in range(TAPS):
                parts = [edge_taps[table, a * HALO + b] * moved[b] for b in range(HALO)]
                edge_acc[e - a + TAPS - 1] += (parts[0] + parts[1]) + parts[2]
            return carry

        lax.fori_loop(HALO, HALO + rows, step, 0, unroll=2)

    def conv_outer(buffer, table, lines):
        for e in lines:
            line = buffer[e].astype(F32)
            for a in range(TAPS):
                if 0 <= e - a < rows:
                    add_line(line, table, e, a)

    def conv_total(start, count):
        edge = edge_acc[pl.ds(TAPS - 1 + start, count)]
        both = jnp.concatenate(
            [jnp.where(lane < EDGE // 2, edge, 0.0), jnp.where(lane < EDGE // 2, 0.0, edge)],
            axis=2,
        )
        return acc[pl.ds(TAPS - 1 + start, count)] + both

    below, above = range(HALO), range(HALO + rows, HALO + rows + HALO)
    settled = rows - HALO

    conv_own(ext, 0)

    loads[3].wait()
    masked_cot = (cot_ref[...] * mask_half[None]).reshape(cells, cols)
    cot_rows[...] = dot(to_rows, masked_cot).astype(BF16).reshape(rows, chans, cols)
    channel_copies(lambda peer: cot_rows.at[peer], cot_all.at[me], 2)

    loads[4].wait()

    full_width = n_lon * cols
    turn = partner_ref[0]
    first = lax.rem(turn - lon * cols - (cols + HALO - 1) + 2 * full_width, full_width)
    first_block = first // cols
    origin = lax.rem(turn - lon * cols + EDGE - first_block * cols + 3 * full_width, full_width)

    @pl.when(lat_last)
    def _():
        source = lax.broadcasted_iota(jnp.int32, (3 * cols, wide), 0)
        want = origin - lax.broadcasted_iota(jnp.int32, (3 * cols, wide), 1)
        want = jnp.where(want < 0, want + full_width, want)
        pick[...] = (source == want).astype(BF16)

    def fold_fill(buffer, gathered):
        found = jnp.zeros((HALO * chans, wide), F32)
        for j in range(3):
            piece = gathered[lax.rem(first_block + j, n_lon)].reshape(HALO * chans, cols)
            found = found + dot(piece, pick[j * cols : (j + 1) * cols, :])
        found = found.astype(BF16).reshape(HALO, chans, wide)
        for j in range(HALO):
            buffer[HALO + rows + j] = found[HALO - 1 - j]

    def square_copy(k):
        turn, flip = square[k]
        piece = weights.at[part, :, mine]
        return pltpu.make_async_remote_copy(
            src_ref=piece,
            dst_ref=piece,
            send_sem=square_send.at[k],
            recv_sem=square_recv.at[k],
            device_id=in_square(turn, flip),
            device_id_type=MESH,
        )

    several(weights.at[part, :, mine], n_ch - 1, 1).wait_recv()
    for k in range(len(square)):
        square_copy(k).start()
    halo_arrived(ext, halo_send, halo_recv)
    unpack_edges(0)
    conv_edges(0)
    conv_outer(ext, 0, below)
    depth_rows[pl.ds(0, settled)] = conv_total(0, settled).astype(BF16)
    channel_copies(
        lambda peer: depth_rows.at[peer], depth_all.at[me], 3, lambda peer: peer < settled
    )

    @pl.when(lat_last)
    def _():
        several(fold_rows, n_lon - 1, 0).wait_recv()
        fold_fill(ext, fold_rows)

    conv_outer(ext, 0, above)
    depth_rows[pl.ds(settled, HALO)] = conv_total(settled, HALO).astype(BF16)
    channel_copies(
        lambda peer: depth_rows.at[peer], depth_all.at[me], 3, lambda peer: peer >= settled
    )

    def swap_weights(half):
        return pltpu.make_async_remote_copy(
            src_ref=weights.at[half],
            dst_ref=weights.at[half],
            send_sem=send.at[4],
            recv_sem=recv.at[4],
            device_id={"lat": sibling, "lon": lon, "ch": me},
            device_id_type=MESH,
        )

    for k in range(len(square)):
        square_copy(k).wait_recv()
    swap_weights(part).start()
    several(cot_all, n_ch, 2).wait_recv()
    several(depth_all, n_ch, 3).wait_recv()

    channels = n_ch * chans
    values = depth_all[...].reshape(channels, cols).astype(F32)
    spread = values - jnp.mean(values, axis=0, keepdims=True)
    inv_scale = lax.rsqrt(jnp.mean(spread * spread, axis=0, keepdims=True) + EPSILON)
    normed_ref[...] = spread * inv_scale
    normed_half = normed_ref[...].astype(BF16)
    cot_here = cot_all[...].reshape(channels, cols)
    swap_weights(1 - part).wait_recv()

    mixed = jnp.zeros((channels, cols), F32)
    back_norm = jnp.zeros((channels, cols), F32)
    per_chunk = n_ch // 4
    for j in range(4):
        span = slice(j * per_chunk, (j + 1) * per_chunk)
        expand = weights[0, span].reshape(per_chunk * hidden_here, channels)
        project = weights[1, span].reshape(per_chunk * hidden_here, channels)
        active, slope = gelu_parts(dot(expand, normed_half))
        back_hidden = (dot(project, cot_here) * slope).astype(BF16)
        mixed = mixed + dot(project, active.astype(BF16), ((0,), (0,)))
        back_norm = back_norm + dot(expand, back_hidden, ((0,), (0,)))
    normed = normed_ref[...]
    mean_plain = jnp.mean(back_norm, axis=0, keepdims=True)
    mean_cross = jnp.mean(back_norm * normed, axis=0, keepdims=True)
    grad_send[...] = (
        (inv_scale * (back_norm - mean_plain - normed * mean_cross))
        .astype(BF16)
        .reshape(n_ch, chans, cols)
    )
    channel_copies(lambda peer: grad_send.at[peer], ext_back.at[HALO + me, :, own_lanes], 5)
    mixed_send[...] = mixed.astype(BF16).reshape(n_ch, chans, cols)
    channel_copies(lambda peer: mixed_send.at[peer], mixed_rows.at[me], 6)

    several(grad_send, n_ch, 5).wait_recv()
    pack_edges(ext_back[own_rows, :, own_lanes].reshape(cells, cols), 1)
    halo_start(ext_back, halo_send_back, halo_recv_back)

    @pl.when(lat_last)
    def _():
        fold_start(ext_back, fold_rows_back, 7)
        fold_rows_back[lon] = ext_back[pl.ds(rows, HALO), :, own_lanes]

    conv_own(ext_back, 1)
    to_chans = (swap_col == lax.rem(swap_row, rows) * chans + swap_row // rows).astype(BF16)
    several(mixed_rows, n_ch, 6).wait_recv()
    mixed_here = dot(to_chans, mixed_rows[...].reshape(cells, cols)).reshape(chans, rows, cols)
    state_sum[...] = (
        mask_ref[...].astype(F32)[None] * (state_ref[...].astype(F32) + mixed_here)
    ).astype(BF16)

    halo_arrived(ext_back, halo_send_back, halo_recv_back)
    unpack_edges(1)
    conv_edges(1)
    conv_outer(ext_back, 1, below)

    @pl.when(lat_last)
    def _():
        several(fold_rows_back, n_lon - 1, 7).wait_recv()
        fold_fill(ext_back, fold_rows_back)

    conv_outer(ext_back, jnp.where(lat_last, 0, 1), above)
    ocean = mask_ref[...].astype(F32)
    grad_rows = (
        cot_rows[...].astype(F32) + ocean[:, None, :] * conv_total(0, rows)
    ).astype(BF16)
    grad_sum[...] = (
        dot(to_chans, grad_rows.reshape(cells, cols)).astype(BF16).reshape(chans, rows, cols)
    )

    halo_sent(ext, halo_send, halo_recv)
    halo_sent(ext_back, halo_send_back, halo_recv_back)

    @pl.when(lat_last)
    def _():
        several(fold_rows, n_lon - 1, 0).wait_send()
        several(fold_rows_back, n_lon - 1, 7).wait_send()

    several(weights.at[part, :, mine], n_ch - 1, 1).wait_send()
    for k in range(len(square)):
        square_copy(k).wait_send()
    several(cot_rows, n_ch, 2).wait_send()
    several(depth_rows, n_ch, 3).wait_send()
    swap_weights(part).wait_send()
    several(grad_send, n_ch, 5).wait_send()
    several(mixed_send, n_ch, 6).wait_send()


def finish_kernel(state_sum, grad_sum, out_ref, grad_ref, sems):
    out_ref[...] = state_sum[...]
    grad_ref[...] = grad_sum[...]


def on_device(state_field, land_mask, partner, kernel, w_expand, w_project, cotangent):
    n_lat, n_lon, n_ch = (lax.axis_size(name) for name in ("lat", "lon", "ch"))
    chans, rows, cols = state_field.shape
    hidden_here = w_project.shape[0]
    assert rows == n_ch and n_lat == 4 and n_lon % 2 == 0 and cols == 2 * EDGE
    wide = cols + 2 * EDGE
    channels = n_ch * chans
    sizes = (n_lat, n_lon, n_ch, rows, chans, cols, hidden_here)
    vmem = pl.BlockSpec(memory_space=pltpu.VMEM)
    tile_rows = rows + 2 * HALO
    state_sum, grad_sum = pl.pallas_call(
        functools.partial(block_kernel, sizes),
        out_shape=(jax.ShapeDtypeStruct(state_field.shape, BF16),) * 2,
        in_specs=[pl.BlockSpec(memory_space=pltpu.HBM)] * 7,
        out_specs=(vmem, vmem),
        scratch_shapes=[
            pltpu.SMEM(partner.shape, jnp.int32),
            pltpu.VMEM(state_field.shape, BF16),
            pltpu.VMEM(land_mask.shape, jnp.int32),
            pltpu.VMEM(kernel.shape, BF16),
            pltpu.VMEM(cotangent.shape, BF16),
            pltpu.VMEM((tile_rows, chans, wide), BF16),
            pltpu.VMEM((tile_rows, chans, wide), BF16),
            pltpu.VMEM((n_lon, HALO, chans, cols), BF16),
            pltpu.VMEM((n_lon, HALO, chans, cols), BF16),
            pltpu.VMEM((3 * cols, wide), BF16),
            pltpu.VMEM((2, TAPS * TAPS, chans, EDGE), F32),
            pltpu.VMEM((rows + 2 * (TAPS - 1), chans, cols), F32),
            pltpu.VMEM((2, TAPS * HALO, chans, EDGE), F32),
            pltpu.VMEM((rows + 2 * (TAPS - 1), chans, EDGE), F32),
            pltpu.VMEM((2, 2, 2 * 8, rows * chans), BF16),
            pltpu.VMEM((2, 2, 2 * 8, rows * chans), BF16),
            pltpu.VMEM((rows, chans, EDGE), F32),
            pltpu.VMEM((rows, chans, cols), BF16),
            pltpu.VMEM((n_ch, chans, cols), BF16),
            pltpu.VMEM((rows, chans, cols), BF16),
            pltpu.VMEM((n_ch, chans, cols), BF16),
            pltpu.VMEM((2, n_ch, hidden_here, channels), BF16),
            pltpu.VMEM((hidden_here // n_lat, channels), BF16),
            pltpu.VMEM((channels, cols), F32),
            pltpu.VMEM((n_ch, chans, cols), BF16),
            pltpu.VMEM((n_ch, chans, cols), BF16),
            pltpu.VMEM((n_ch, chans, cols), BF16),
            pltpu.SemaphoreType.DMA((8,)),
            pltpu.SemaphoreType.DMA((8,)),
            pltpu.SemaphoreType.DMA((8,)),
            pltpu.SemaphoreType.DMA((8,)),
            pltpu.SemaphoreType.DMA((8,)),
            pltpu.SemaphoreType.DMA((8,)),
            pltpu.SemaphoreType.DMA((n_lat - 1,)),
            pltpu.SemaphoreType.DMA((n_lat - 1,)),
            pltpu.SemaphoreType.DMA((7,)),
        ],
        compiler_params=pltpu.CompilerParams(
            collective_id=0, has_side_effects=True, vmem_limit_bytes=64 * 1000 * 1000
        ),
        name="ocean_block",
    )(partner, state_field, land_mask, kernel, w_expand.T, w_project, cotangent)
    anywhere = pl.BlockSpec(memory_space=pltpu.VMEM)
    return pl.pallas_call(
        finish_kernel,
        out_shape=(jax.ShapeDtypeStruct(state_field.shape, BF16),) * 2,
        in_specs=[anywhere] * 2,
        out_specs=(anywhere, anywhere),
        scratch_shapes=[pltpu.SemaphoreType.DMA((2,))],
        name="finish",
    )(state_sum, grad_sum)


def solution(mesh):
    placed = (
        P("ch", "lat", "lon"),
        P("lat", "lon"),
        P(),
        P("ch", None),
        P(None, "ch"),
        P("ch", None),
        P("ch", "lat", "lon"),
    )
    return jax.shard_map(
        on_device,
        mesh=mesh,
        in_specs=placed,
        out_specs=(P("ch", "lat", "lon"), P("ch", "lat", "lon")),
        check_vma=False,
    )
```

```python
import functools

import jax
import jax.numpy as jnp
from jax import lax
from jax.experimental import pallas as pl
from jax.experimental.pallas import tpu as pltpu
from jax.sharding import PartitionSpec as P

EPSILON = 1e-06
HALO = 3
EDGE = 128
TAPS = 7
DIRECTIONS = ((-1, 0), (1, 0), (0, -1), (0, 1), (-1, -1), (-1, 1), (1, -1), (1, 1))
MESH = pl.DeviceIdType.MESH
F32 = jnp.float32
BF16 = jnp.bfloat16


def dot(a, b, dims=((1,), (0,))):
    return lax.dot_general(a, b, (dims, ((), ())), preferred_element_type=F32)


def gelu_parts(hidden):
    normal_cdf = 0.5 * (1.0 + lax.erf(hidden * 0.7071067811865476))
    return (
        hidden * normal_cdf,
        normal_cdf + hidden * jnp.exp(-0.5 * hidden * hidden) * 0.3989422804014327,
    )


def block_kernel(
    sizes,
    partner_hbm,
    state_hbm,
    mask_hbm,
    kernel_hbm,
    expand_hbm,
    project_hbm,
    cot_hbm,
    state_sum,
    grad_sum,
    partner_ref,
    state_ref,
    mask_ref,
    kernel_ref,
    cot_ref,
    ext,
    ext_back,
    fold_rows,
    fold_rows_back,
    pick,
    taps,
    acc,
    edge_taps,
    edge_acc,
    edge_out,
    edge_in,
    edge_tile,
    cot_rows,
    cot_all,
    depth_rows,
    depth_all,
    weights,
    weights_send,
    normed_ref,
    active_half,
    mixed_send,
    grad_send,
    mixed_rows,
    halo_send,
    halo_recv,
    halo_send_back,
    halo_recv_back,
    send,
    recv,
    square_send,
    square_recv,
    load,
):
    n_lat, n_lon, n_ch, rows, chans, cols, hidden_here = sizes
    wide = cols + 2 * EDGE
    cells = rows * chans
    lat, lon, me = lax.axis_index("lat"), lax.axis_index("lon"), lax.axis_index("ch")
    lat_last = lat == n_lat - 1
    part = lax.rem(lat, 2)
    sibling = lat + 1 - 2 * part
    pairs = n_lat // 2
    share = hidden_here // (2 * pairs)
    across = lax.rem(lat + pairs, n_lat)

    def share_of(row_block):
        index = row_block // 2 * 2 + lax.rem(lon, 2)
        return pl.ds(pl.multiple_of(index * share, share), share)

    mine, given = share_of(across), share_of(lat)
    lon_twin = lon + 1 - 2 * lax.rem(lon, 2)
    square = [(0, 1)] + [(2 * i, j) for i in range(1, pairs) for j in (0, 1)]

    def in_square(turn, flip):
        return {
            "lat": lax.rem(lat + turn, n_lat),
            "lon": lon_twin if flip else lon,
            "ch": me,
        }
    own_rows = pl.ds(HALO, rows)
    own_lanes = pl.ds(EDGE, cols)

    def exists(dl):
        return jnp.logical_and(lat + dl >= 0, lat + dl < n_lat)

    def at(dl, do):
        return {"lat": lat + dl, "lon": lax.rem(lon + do + n_lon, n_lon), "ch": me}

    barrier = pltpu.get_barrier_semaphore()

    def greet_channel(i, carry):
        pl.semaphore_signal(
            barrier,
            device_id={"lat": across, "lon": lon, "ch": i},
            device_id_type=MESH,
        )
        return carry

    def greet_fold(i, carry):
        pl.semaphore_signal(
            barrier,
            device_id={"lat": lat, "lon": lax.rem(lon + i, n_lon), "ch": me},
            device_id_type=MESH,
        )
        return carry

    for dl, do in DIRECTIONS:

        @pl.when(exists(dl))
        def _():
            pl.semaphore_signal(barrier, device_id=at(dl, do), device_id_type=MESH)

    lax.fori_loop(0, n_ch, greet_channel, 0)
    for turn, flip in square[1:]:
        if (turn, flip) == (pairs, 0):
            continue
        pl.semaphore_signal(barrier, device_id=in_square(turn, flip), device_id_type=MESH)

    @pl.when(lat_last)
    def _():
        lax.fori_loop(1, n_lon, greet_fold, 0)

    def fetch(k, src, dst):
        return pltpu.make_async_copy(src, dst, load.at[k])

    loads = [
        fetch(0, state_hbm, state_ref),
        fetch(1, mask_hbm, mask_ref),
        fetch(2, kernel_hbm, kernel_ref),
        fetch(3, cot_hbm, cot_ref),
        fetch(4, partner_hbm, partner_ref),
    ]
    own_expand = [
        fetch(5, expand_hbm.at[mine], weights.at[0, me, mine]),
        fetch(6, expand_hbm.at[given], weights_send),
    ]
    own_project = [
        fetch(5, project_hbm.at[mine], weights.at[1, me, mine]),
        fetch(6, project_hbm.at[given], weights_send),
    ]
    for copy in loads:
        copy.start()

    @pl.when(part == 0)
    def _():
        for copy in own_expand:
            copy.start()

    @pl.when(part == 1)
    def _():
        for copy in own_project:
            copy.start()

    swap_row = lax.broadcasted_iota(jnp.int32, (cells, cells), 0)
    swap_col = lax.broadcasted_iota(jnp.int32, (cells, cells), 1)
    to_rows = (swap_col == lax.rem(swap_row, chans) * rows + swap_row // chans).astype(BF16)
    loads[0].wait()
    loads[1].wait()
    mask_half = mask_ref[...].astype(BF16)
    masked = (state_ref[...] * mask_half[None]).reshape(cells, cols)
    own_cells = dot(to_rows, masked).astype(BF16)
    ext[own_rows, :, own_lanes] = own_cells.reshape(rows, chans, cols)

    slot = lax.broadcasted_iota(jnp.int32, (2 * 8, EDGE), 0)
    spot = lax.broadcasted_iota(jnp.int32, (2 * 8, EDGE), 1)
    first_cols = jnp.logical_and(slot < HALO, spot == slot).astype(BF16)
    last_cols = jnp.logical_and(slot < HALO, spot == slot + EDGE - HALO).astype(BF16)

    def pack_edges(block, phase):
        edge_out[phase, 0] = dot(first_cols, block[:, :EDGE], ((1,), (1,))).astype(BF16)
        edge_out[phase, 1] = dot(last_cols, block[:, cols - EDGE :], ((1,), (1,))).astype(BF16)

    def unpack_edges(phase):
        both = dot(edge_in[phase, 0], last_cols, ((0,), (0,))) + dot(
            edge_in[phase, 1], first_cols, ((0,), (0,))
        )
        edge_tile[...] = both.reshape(rows, chans, EDGE)

    pack_edges(own_cells, 0)
    @pl.when(lat == 0)
    def _():
        ext[0:HALO] = jnp.zeros((HALO, chans, wide), BF16)
        ext_back[0:HALO] = jnp.zeros((HALO, chans, wide), BF16)

    @pl.when(lat_last)
    def _():
        fold_rows[lon] = ext[pl.ds(rows, HALO), :, own_lanes]

    for copy in own_expand:
        copy.wait()
    neighbours = sum(
        (exists(dl).astype(jnp.int32) for dl, _ in DIRECTIONS), jnp.int32(n_ch + len(square) - 2)
    ) + jnp.where(lat_last, n_lon - 1, 0)
    pl.semaphore_wait(barrier, neighbours)

    def halo_copy(buffer, d, send_sems, recv_sems):
        dl, do = DIRECTIONS[d]
        if dl == 0:
            phase = 0 if buffer is ext else 1
            return pltpu.make_async_remote_copy(
                src_ref=edge_out.at[phase, (1 + do) // 2],
                dst_ref=edge_in.at[phase, (1 - do) // 2],
                send_sem=send_sems.at[d],
                recv_sem=recv_sems.at[d],
                device_id=at(dl, do),
                device_id_type=MESH,
            )
        src_rows, dst_rows = {
            -1: (pl.ds(HALO, HALO), pl.ds(HALO + rows, HALO)),
            1: (pl.ds(rows, HALO), pl.ds(0, HALO)),
        }[dl]
        src_lanes, dst_lanes = {
            -1: (pl.ds(EDGE, EDGE), pl.ds(EDGE + cols, EDGE)),
            0: (own_lanes, own_lanes),
            1: (pl.ds(cols, EDGE), pl.ds(0, EDGE)),
        }[do]
        return pltpu.make_async_remote_copy(
            src_ref=buffer.at[src_rows, :, src_lanes],
            dst_ref=buffer.at[dst_rows, :, dst_lanes],
            send_sem=send_sems.at[d],
            recv_sem=recv_sems.at[d],
            device_id=at(dl, do),
            device_id_type=MESH,
        )

    def halo_start(buffer, send_sems, recv_sems):
        for d, (dl, _) in enumerate(DIRECTIONS):
            pl.when(exists(dl))(lambda d=d: halo_copy(buffer, d, send_sems, recv_sems).start())

    def halo_arrived(buffer, send_sems, recv_sems):
        for d, (dl, _) in enumerate(DIRECTIONS):
            pl.when(exists(-dl))(
                lambda d=d: halo_copy(buffer, d, send_sems, recv_sems).wait_recv()
            )

    def halo_sent(buffer, send_sems, recv_sems):
        for d, (dl, _) in enumerate(DIRECTIONS):
            pl.when(exists(dl))(
                lambda d=d: halo_copy(buffer, d, send_sems, recv_sems).wait_send()
            )

    def fold_copy(buffer, gathered, i, k):
        return pltpu.make_async_remote_copy(
            src_ref=buffer.at[pl.ds(rows, HALO), :, own_lanes],
            dst_ref=gathered.at[lon],
            send_sem=send.at[k],
            recv_sem=recv.at[k],
            device_id={"lat": lat, "lon": lax.rem(lon + i, n_lon), "ch": me},
            device_id_type=MESH,
        )

    def several(gathered, count, k):
        whole = gathered.at[pl.ds(0, count)]
        return pltpu.make_async_remote_copy(
            src_ref=whole,
            dst_ref=whole,
            send_sem=send.at[k],
            recv_sem=recv.at[k],
            device_id={"lat": across, "lon": lon, "ch": me},
            device_id_type=MESH,
        )

    def channel_copies(make_src, dst, k, wanted=None):
        def step(j, carry):
            away = (j + 1) // 2
            peer = lax.rem(me + n_ch // 2 + n_ch + away * (1 - 2 * lax.rem(j, 2)), n_ch)

            def go():
                pltpu.make_async_remote_copy(
                    src_ref=make_src(peer),
                    dst_ref=dst,
                    send_sem=send.at[k],
                    recv_sem=recv.at[k],
                    device_id={"lat": across, "lon": lon, "ch": peer},
                    device_id_type=MESH,
                ).start()

            if wanted is None:
                go()
            else:
                pl.when(wanted(peer))(go)
            return carry

        lax.fori_loop(0, n_ch, step, 0)

    def fold_start(buffer, gathered, k):
        def step(j, carry):
            away = (j + 1) // 2
            i = n_lon // 2 + away * (1 - 2 * lax.rem(j, 2))
            fold_copy(buffer, gathered, i, k).start()
            return carry

        lax.fori_loop(0, n_lon - 1, step, 0)

    halo_start(ext, halo_send, halo_recv)

    @pl.when(lat_last)
    def _():
        fold_start(ext, fold_rows, 0)

    channel_copies(
        lambda peer: weights_send, weights.at[part, me, given], 1, lambda peer: peer != me
    )
    loads[2].wait()
    for t in range(TAPS * TAPS):
        tap = jnp.broadcast_to(kernel_ref[:, t : t + 1].astype(F32), (chans, EDGE))
        taps[0, t] = tap
        taps[1, TAPS * TAPS - 1 - t] = tap
    lane = lax.broadcasted_iota(jnp.int32, (chans, EDGE), 1)
    for table in range(2):
        for a in range(TAPS):
            for b in range(HALO):
                edge_taps[table, a * HALO + b] = jnp.where(
                    lane < EDGE // 2,
                    taps[table, a * TAPS + b],
                    taps[table, a * TAPS + b + HALO + 1],
                )

    def add_line(line, table, e, a):
        parts = [
            jnp.concatenate([taps[table, a * TAPS + b]] * (cols // EDGE), axis=1)
            * line[:, EDGE - HALO + b : EDGE - HALO + b + cols]
            for b in range(TAPS)
        ]
        acc[e - a + TAPS - 1] += ((parts[0] + parts[1]) + (parts[2] + parts[3])) + (
            (parts[4] + parts[5]) + parts[6]
        )

    def conv_own(buffer, table):
        acc[...] = jnp.zeros(acc.shape, F32)
        edge_acc[...] = jnp.zeros(edge_acc.shape, F32)
        blank = jnp.zeros((chans, EDGE), F32)

        def step(e, carry):
            own = buffer[e, :, own_lanes].astype(F32)
            line = jnp.concatenate([blank, own, blank], axis=1)
            for a in range(TAPS):
                add_line(line, table, e, a)
            return carry

        lax.fori_loop(HALO, HALO + rows, step, 0, unroll=2)

    def conv_edges(table):
        def step(e, carry):
            tile = edge_tile[e - HALO]
            left = jnp.where(lane >= EDGE // 2, tile, 0.0)
            right = jnp.where(lane < EDGE // 2, tile, 0.0)
            moved = [
                jnp.where(
                    lane < EDGE // 2,
                    pltpu.roll(left, HALO - b, 1),
                    pltpu.roll(right, EDGE - 1 - b, 1),
                )
                for b in range(HALO)
            ]
            for a in range(TAPS):
                parts = [edge_taps[table, a * HALO + b] * moved[b] for b in range(HALO)]
                edge_acc[e - a + TAPS - 1] += (parts[0] + parts[1]) + parts[2]
            return carry

        lax.fori_loop(HALO, HALO + rows, step, 0, unroll=2)

    def conv_outer(buffer, table, lines):
        for e in lines:
            line = buffer[e].astype(F32)
            for a in range(TAPS):
                if 0 <= e - a < rows:
                    add_line(line, table, e, a)

    def conv_total(start, count):
        edge = edge_acc[pl.ds(TAPS - 1 + start, count)]
        both = jnp.concatenate(
            [jnp.where(lane < EDGE // 2, edge, 0.0), jnp.where(lane < EDGE // 2, 0.0, edge)],
            axis=2,
        )
        return acc[pl.ds(TAPS - 1 + start, count)] + both

    below, above = range(HALO), range(HALO + rows, HALO + rows + HALO)
    settled = rows - HALO

    conv_own(ext, 0)

    loads[3].wait()
    masked_cot = (cot_ref[...] * mask_half[None]).reshape(cells, cols)
    cot_rows[...] = dot(to_rows, masked_cot).astype(BF16).reshape(rows, chans, cols)
    channel_copies(lambda peer: cot_rows.at[peer], cot_all.at[me], 2)

    loads[4].wait()

    full_width = n_lon * cols
    turn = partner_ref[0]
    first = lax.rem(turn - lon * cols - (cols + HALO - 1) + 2 * full_width, full_width)
    first_block = first // cols
    origin = lax.rem(turn - lon * cols + EDGE - first_block * cols + 3 * full_width, full_width)

    @pl.when(lat_last)
    def _():
        source = lax.broadcasted_iota(jnp.int32, (3 * cols, wide), 0)
        want = origin - lax.broadcasted_iota(jnp.int32, (3 * cols, wide), 1)
        want = jnp.where(want < 0, want + full_width, want)
        pick[...] = (source == want).astype(BF16)

    def fold_fill(buffer, gathered):
        found = jnp.zeros((HALO * chans, wide), F32)
        for j in range(3):
            piece = gathered[lax.rem(first_block + j, n_lon)].reshape(HALO * chans, cols)
            found = found + dot(piece, pick[j * cols : (j + 1) * cols, :])
        found = found.astype(BF16).reshape(HALO, chans, wide)
        for j in range(HALO):
            buffer[HALO + rows + j] = found[HALO - 1 - j]

    def square_copy(k):
        turn, flip = square[k]
        piece = weights.at[part, :, mine]
        return pltpu.make_async_remote_copy(
            src_ref=piece,
            dst_ref=piece,
            send_sem=square_send.at[k],
            recv_sem=square_recv.at[k],
            device_id=in_square(turn, flip),
            device_id_type=MESH,
        )

    several(weights.at[part, :, mine], n_ch - 1, 1).wait_recv()
    for k in range(len(square)):
        square_copy(k).start()
    halo_arrived(ext, halo_send, halo_recv)
    unpack_edges(0)
    conv_edges(0)
    conv_outer(ext, 0, below)
    depth_rows[pl.ds(0, settled)] = conv_total(0, settled).astype(BF16)
    channel_copies(
        lambda peer: depth_rows.at[peer], depth_all.at[me], 3, lambda peer: peer < settled
    )

    @pl.when(lat_last)
    def _():
        several(fold_rows, n_lon - 1, 0).wait_recv()
        fold_fill(ext, fold_rows)

    conv_outer(ext, 0, above)
    depth_rows[pl.ds(settled, HALO)] = conv_total(settled, HALO).astype(BF16)
    channel_copies(
        lambda peer: depth_rows.at[peer], depth_all.at[me], 3, lambda peer: peer >= settled
    )

    def swap_weights(half):
        return pltpu.make_async_remote_copy(
            src_ref=weights.at[half],
            dst_ref=weights.at[half],
            send_sem=send.at[4],
            recv_sem=recv.at[4],
            device_id={"lat": sibling, "lon": lon, "ch": me},
            device_id_type=MESH,
        )

    for k in range(len(square)):
        square_copy(k).wait_recv()
    swap_weights(part).start()
    several(cot_all, n_ch, 2).wait_recv()
    several(depth_all, n_ch, 3).wait_recv()

    channels = n_ch * chans
    values = depth_all[...].reshape(channels, cols).astype(F32)
    spread = values - jnp.mean(values, axis=0, keepdims=True)
    inv_scale = lax.rsqrt(jnp.mean(spread * spread, axis=0, keepdims=True) + EPSILON)
    normed_ref[...] = spread * inv_scale
    normed_half = normed_ref[...].astype(BF16)
    cot_here = cot_all[...].reshape(channels, cols)
    swap_weights(1 - part).wait_recv()

    back_norm = jnp.zeros((channels, cols), F32)
    per_chunk = n_ch // 4
    chunk = per_chunk * hidden_here
    chunks = [slice(j * per_chunk, (j + 1) * per_chunk) for j in range(4)]
    for j, span in enumerate(chunks):
        expand = weights[0, span].reshape(chunk, channels)
        project = weights[1, span].reshape(chunk, channels)
        active, slope = gelu_parts(dot(expand, normed_half))
        active_half[j] = active.astype(BF16)
        back_hidden = (dot(project, cot_here) * slope).astype(BF16)
        back_norm = back_norm + dot(expand, back_hidden, ((0,), (0,)))
    normed = normed_ref[...]
    mean_plain = jnp.mean(back_norm, axis=0, keepdims=True)
    mean_cross = jnp.mean(back_norm * normed, axis=0, keepdims=True)
    grad_send[...] = (
        (inv_scale * (back_norm - mean_plain - normed * mean_cross))
        .astype(BF16)
        .reshape(n_ch, chans, cols)
    )
    channel_copies(lambda peer: grad_send.at[peer], ext_back.at[HALO + me, :, own_lanes], 5)
    mixed = jnp.zeros((channels, cols), F32)
    for j, span in enumerate(chunks):
        mixed = mixed + dot(
            weights[1, span].reshape(chunk, channels), active_half[j], ((0,), (0,))
        )
    mixed_send[...] = mixed.astype(BF16).reshape(n_ch, chans, cols)

    several(grad_send, n_ch, 5).wait_recv()
    pack_edges(ext_back[own_rows, :, own_lanes].reshape(cells, cols), 1)
    halo_start(ext_back, halo_send_back, halo_recv_back)

    @pl.when(lat_last)
    def _():
        fold_start(ext_back, fold_rows_back, 7)
        fold_rows_back[lon] = ext_back[pl.ds(rows, HALO), :, own_lanes]

    channel_copies(lambda peer: mixed_send.at[peer], mixed_rows.at[me], 6)
    conv_own(ext_back, 1)
    halo_arrived(ext_back, halo_send_back, halo_recv_back)
    unpack_edges(1)
    conv_edges(1)
    conv_outer(ext_back, 1, below)
    to_chans = (swap_col == lax.rem(swap_row, rows) * chans + swap_row // rows).astype(BF16)
    several(mixed_rows, n_ch, 6).wait_recv()
    mixed_here = dot(to_chans, mixed_rows[...].reshape(cells, cols)).reshape(chans, rows, cols)
    state_sum[...] = (
        mask_ref[...].astype(F32)[None] * (state_ref[...].astype(F32) + mixed_here)
    ).astype(BF16)

    @pl.when(lat_last)
    def _():
        several(fold_rows_back, n_lon - 1, 7).wait_recv()
        fold_fill(ext_back, fold_rows_back)

    conv_outer(ext_back, jnp.where(lat_last, 0, 1), above)
    ocean = mask_ref[...].astype(F32)
    grad_rows = (
        cot_rows[...].astype(F32) + ocean[:, None, :] * conv_total(0, rows)
    ).astype(BF16)
    grad_sum[...] = (
        dot(to_chans, grad_rows.reshape(cells, cols)).astype(BF16).reshape(chans, rows, cols)
    )

    halo_sent(ext, halo_send, halo_recv)
    halo_sent(ext_back, halo_send_back, halo_recv_back)

    @pl.when(lat_last)
    def _():
        several(fold_rows, n_lon - 1, 0).wait_send()
        several(fold_rows_back, n_lon - 1, 7).wait_send()

    several(weights.at[part, :, mine], n_ch - 1, 1).wait_send()
    for k in range(len(square)):
        square_copy(k).wait_send()
    several(cot_rows, n_ch, 2).wait_send()
    several(depth_rows, n_ch, 3).wait_send()
    swap_weights(part).wait_send()
    several(grad_send, n_ch, 5).wait_send()
    several(mixed_send, n_ch, 6).wait_send()


def finish_kernel(state_sum, grad_sum, out_ref, grad_ref, sems):
    out_ref[...] = state_sum[...]
    grad_ref[...] = grad_sum[...]


def on_device(state_field, land_mask, partner, kernel, w_expand, w_project, cotangent):
    n_lat, n_lon, n_ch = (lax.axis_size(name) for name in ("lat", "lon", "ch"))
    chans, rows, cols = state_field.shape
    hidden_here = w_project.shape[0]
    assert rows == n_ch and n_lat == 4 and n_lon % 2 == 0 and cols == 2 * EDGE
    wide = cols + 2 * EDGE
    channels = n_ch * chans
    sizes = (n_lat, n_lon, n_ch, rows, chans, cols, hidden_here)
    vmem = pl.BlockSpec(memory_space=pltpu.VMEM)
    tile_rows = rows + 2 * HALO
    state_sum, grad_sum = pl.pallas_call(
        functools.partial(block_kernel, sizes),
        out_shape=(jax.ShapeDtypeStruct(state_field.shape, BF16),) * 2,
        in_specs=[pl.BlockSpec(memory_space=pltpu.HBM)] * 7,
        out_specs=(vmem, vmem),
        scratch_shapes=[
            pltpu.SMEM(partner.shape, jnp.int32),
            pltpu.VMEM(state_field.shape, BF16),
            pltpu.VMEM(land_mask.shape, jnp.int32),
            pltpu.VMEM(kernel.shape, BF16),
            pltpu.VMEM(cotangent.shape, BF16),
            pltpu.VMEM((tile_rows, chans, wide), BF16),
            pltpu.VMEM((tile_rows, chans, wide), BF16),
            pltpu.VMEM((n_lon, HALO, chans, cols), BF16),
            pltpu.VMEM((n_lon, HALO, chans, cols), BF16),
            pltpu.VMEM((3 * cols, wide), BF16),
            pltpu.VMEM((2, TAPS * TAPS, chans, EDGE), F32),
            pltpu.VMEM((rows + 2 * (TAPS - 1), chans, cols), F32),
            pltpu.VMEM((2, TAPS * HALO, chans, EDGE), F32),
            pltpu.VMEM((rows + 2 * (TAPS - 1), chans, EDGE), F32),
            pltpu.VMEM((2, 2, 2 * 8, rows * chans), BF16),
            pltpu.VMEM((2, 2, 2 * 8, rows * chans), BF16),
            pltpu.VMEM((rows, chans, EDGE), F32),
            pltpu.VMEM((rows, chans, cols), BF16),
            pltpu.VMEM((n_ch, chans, cols), BF16),
            pltpu.VMEM((rows, chans, cols), BF16),
            pltpu.VMEM((n_ch, chans, cols), BF16),
            pltpu.VMEM((2, n_ch, hidden_here, channels), BF16),
            pltpu.VMEM((hidden_here // n_lat, channels), BF16),
            pltpu.VMEM((channels, cols), F32),
            pltpu.VMEM((4, n_ch // 4 * hidden_here, cols), BF16),
            pltpu.VMEM((n_ch, chans, cols), BF16),
            pltpu.VMEM((n_ch, chans, cols), BF16),
            pltpu.VMEM((n_ch, chans, cols), BF16),
            pltpu.SemaphoreType.DMA((8,)),
            pltpu.SemaphoreType.DMA((8,)),
            pltpu.SemaphoreType.DMA((8,)),
            pltpu.SemaphoreType.DMA((8,)),
            pltpu.SemaphoreType.DMA((8,)),
            pltpu.SemaphoreType.DMA((8,)),
            pltpu.SemaphoreType.DMA((n_lat - 1,)),
            pltpu.SemaphoreType.DMA((n_lat - 1,)),
            pltpu.SemaphoreType.DMA((7,)),
        ],
        compiler_params=pltpu.CompilerParams(
            collective_id=0, has_side_effects=True, vmem_limit_bytes=64 * 1000 * 1000
        ),
        name="ocean_block",
    )(partner, state_field, land_mask, kernel, w_expand.T, w_project, cotangent)
    anywhere = pl.BlockSpec(memory_space=pltpu.VMEM)
    return pl.pallas_call(
        finish_kernel,
        out_shape=(jax.ShapeDtypeStruct(state_field.shape, BF16),) * 2,
        in_specs=[anywhere] * 2,
        out_specs=(anywhere, anywhere),
        scratch_shapes=[pltpu.SemaphoreType.DMA((2,))],
        name="finish",
    )(state_sum, grad_sum)


def solution(mesh):
    placed = (
        P("ch", "lat", "lon"),
        P("lat", "lon"),
        P(),
        P("ch", None),
        P(None, "ch"),
        P("ch", None),
        P("ch", "lat", "lon"),
    )
    return jax.shard_map(
        on_device,
        mesh=mesh,
        in_specs=placed,
        out_specs=(P("ch", "lat", "lon"), P("ch", "lat", "lon")),
        check_vma=False,
    )
```

```python
import functools

import jax
import jax.numpy as jnp
from jax import lax
from jax.experimental import pallas as pl
from jax.experimental.pallas import tpu as pltpu
from jax.sharding import PartitionSpec as P

EPSILON = 1e-06
HALO = 3
EDGE = 128
TAPS = 7
DIRECTIONS = ((-1, 0), (1, 0), (0, -1), (0, 1), (-1, -1), (-1, 1), (1, -1), (1, 1))
MESH = pl.DeviceIdType.MESH
F32 = jnp.float32
BF16 = jnp.bfloat16


def dot(a, b, dims=((1,), (0,))):
    return lax.dot_general(a, b, (dims, ((), ())), preferred_element_type=F32)


def gelu_parts(hidden):
    normal_cdf = 0.5 * (1.0 + lax.erf(hidden * 0.7071067811865476))
    return (
        hidden * normal_cdf,
        normal_cdf + hidden * jnp.exp(-0.5 * hidden * hidden) * 0.3989422804014327,
    )


def block_kernel(
    sizes,
    partner_hbm,
    state_hbm,
    mask_hbm,
    kernel_hbm,
    expand_hbm,
    project_hbm,
    cot_hbm,
    state_sum,
    grad_sum,
    partner_ref,
    state_ref,
    mask_ref,
    kernel_ref,
    cot_ref,
    ext,
    ext_back,
    fold_rows,
    fold_rows_back,
    pick,
    taps,
    acc,
    edge_taps,
    edge_acc,
    edge_out,
    edge_in,
    edge_tile,
    cot_rows,
    cot_all,
    depth_rows,
    depth_all,
    weights,
    weights_send,
    normed_ref,
    active_half,
    mixed_send,
    grad_send,
    mixed_rows,
    halo_send,
    halo_recv,
    halo_send_back,
    halo_recv_back,
    send,
    recv,
    square_send,
    square_recv,
    load,
):
    n_lat, n_lon, n_ch, rows, chans, cols, hidden_here = sizes
    wide = cols + 2 * EDGE
    cells = rows * chans
    lat, lon, me = lax.axis_index("lat"), lax.axis_index("lon"), lax.axis_index("ch")
    lat_last = lat == n_lat - 1
    part = lax.rem(lat, 2)
    sibling = lat + 1 - 2 * part
    pairs = n_lat // 2
    share = hidden_here // (2 * pairs)
    across = lax.rem(lat + pairs, n_lat)

    def share_of(row_block):
        index = row_block // 2 * 2 + lax.rem(lon, 2)
        return pl.ds(pl.multiple_of(index * share, share), share)

    mine, given = share_of(across), share_of(lat)
    lon_twin = lon + 1 - 2 * lax.rem(lon, 2)
    square = [(2 * i, j) for i in range(1, pairs) for j in (1, 0)] + [(0, 1)]

    def in_square(turn, flip):
        return {
            "lat": lax.rem(lat + turn, n_lat),
            "lon": lon_twin if flip else lon,
            "ch": me,
        }
    own_rows = pl.ds(HALO, rows)
    own_lanes = pl.ds(EDGE, cols)

    def exists(dl):
        return jnp.logical_and(lat + dl >= 0, lat + dl < n_lat)

    def at(dl, do):
        return {"lat": lat + dl, "lon": lax.rem(lon + do + n_lon, n_lon), "ch": me}

    barrier = pltpu.get_barrier_semaphore()

    def greet_channel(i, carry):
        pl.semaphore_signal(
            barrier,
            device_id={"lat": across, "lon": lon, "ch": i},
            device_id_type=MESH,
        )
        return carry

    def greet_fold(i, carry):
        pl.semaphore_signal(
            barrier,
            device_id={"lat": lat, "lon": lax.rem(lon + i, n_lon), "ch": me},
            device_id_type=MESH,
        )
        return carry

    for dl, do in DIRECTIONS:

        @pl.when(exists(dl))
        def _():
            pl.semaphore_signal(barrier, device_id=at(dl, do), device_id_type=MESH)

    lax.fori_loop(0, n_ch, greet_channel, 0)
    for turn, flip in square[:-1]:
        if (turn, flip) == (pairs, 0):
            continue
        pl.semaphore_signal(barrier, device_id=in_square(turn, flip), device_id_type=MESH)

    @pl.when(lat_last)
    def _():
        lax.fori_loop(1, n_lon, greet_fold, 0)

    def fetch(k, src, dst):
        return pltpu.make_async_copy(src, dst, load.at[k])

    loads = [
        fetch(0, state_hbm, state_ref),
        fetch(1, mask_hbm, mask_ref),
        fetch(2, kernel_hbm, kernel_ref),
        fetch(3, cot_hbm, cot_ref),
        fetch(4, partner_hbm, partner_ref),
    ]
    own_expand = [
        fetch(5, expand_hbm.at[mine], weights.at[0, me, mine]),
        fetch(6, expand_hbm.at[given], weights_send),
    ]
    own_project = [
        fetch(5, project_hbm.at[mine], weights.at[1, me, mine]),
        fetch(6, project_hbm.at[given], weights_send),
    ]
    for copy in loads:
        copy.start()

    @pl.when(part == 0)
    def _():
        for copy in own_expand:
            copy.start()

    @pl.when(part == 1)
    def _():
        for copy in own_project:
            copy.start()

    swap_row = lax.broadcasted_iota(jnp.int32, (cells, cells), 0)
    swap_col = lax.broadcasted_iota(jnp.int32, (cells, cells), 1)
    to_rows = (swap_col == lax.rem(swap_row, chans) * rows + swap_row // chans).astype(BF16)
    loads[0].wait()
    loads[1].wait()
    mask_half = mask_ref[...].astype(BF16)
    masked = (state_ref[...] * mask_half[None]).reshape(cells, cols)
    own_cells = dot(to_rows, masked).astype(BF16)
    ext[own_rows, :, own_lanes] = own_cells.reshape(rows, chans, cols)

    slot = lax.broadcasted_iota(jnp.int32, (2 * 8, EDGE), 0)
    spot = lax.broadcasted_iota(jnp.int32, (2 * 8, EDGE), 1)
    first_cols = jnp.logical_and(slot < HALO, spot == slot).astype(BF16)
    last_cols = jnp.logical_and(slot < HALO, spot == slot + EDGE - HALO).astype(BF16)

    def pack_edges(block, phase):
        edge_out[phase, 0] = dot(first_cols, block[:, :EDGE], ((1,), (1,))).astype(BF16)
        edge_out[phase, 1] = dot(last_cols, block[:, cols - EDGE :], ((1,), (1,))).astype(BF16)

    def unpack_edges(phase):
        both = dot(edge_in[phase, 0], last_cols, ((0,), (0,))) + dot(
            edge_in[phase, 1], first_cols, ((0,), (0,))
        )
        edge_tile[...] = both.reshape(rows, chans, EDGE)

    pack_edges(own_cells, 0)
    @pl.when(lat == 0)
    def _():
        ext[0:HALO] = jnp.zeros((HALO, chans, wide), BF16)
        ext_back[0:HALO] = jnp.zeros((HALO, chans, wide), BF16)

    @pl.when(lat_last)
    def _():
        fold_rows[lon] = ext[pl.ds(rows, HALO), :, own_lanes]

    for copy in own_expand:
        copy.wait()
    neighbours = sum(
        (exists(dl).astype(jnp.int32) for dl, _ in DIRECTIONS), jnp.int32(n_ch + len(square) - 2)
    ) + jnp.where(lat_last, n_lon - 1, 0)
    pl.semaphore_wait(barrier, neighbours)

    def halo_copy(buffer, d, send_sems, recv_sems):
        dl, do = DIRECTIONS[d]
        if dl == 0:
            phase = 0 if buffer is ext else 1
            return pltpu.make_async_remote_copy(
                src_ref=edge_out.at[phase, (1 + do) // 2],
                dst_ref=edge_in.at[phase, (1 - do) // 2],
                send_sem=send_sems.at[d],
                recv_sem=recv_sems.at[d],
                device_id=at(dl, do),
                device_id_type=MESH,
            )
        src_rows, dst_rows = {
            -1: (pl.ds(HALO, HALO), pl.ds(HALO + rows, HALO)),
            1: (pl.ds(rows, HALO), pl.ds(0, HALO)),
        }[dl]
        src_lanes, dst_lanes = {
            -1: (pl.ds(EDGE, EDGE), pl.ds(EDGE + cols, EDGE)),
            0: (own_lanes, own_lanes),
            1: (pl.ds(cols, EDGE), pl.ds(0, EDGE)),
        }[do]
        return pltpu.make_async_remote_copy(
            src_ref=buffer.at[src_rows, :, src_lanes],
            dst_ref=buffer.at[dst_rows, :, dst_lanes],
            send_sem=send_sems.at[d],
            recv_sem=recv_sems.at[d],
            device_id=at(dl, do),
            device_id_type=MESH,
        )

    def halo_start(buffer, send_sems, recv_sems):
        for d, (dl, _) in enumerate(DIRECTIONS):
            pl.when(exists(dl))(lambda d=d: halo_copy(buffer, d, send_sems, recv_sems).start())

    def halo_arrived(buffer, send_sems, recv_sems):
        for d, (dl, _) in enumerate(DIRECTIONS):
            pl.when(exists(-dl))(
                lambda d=d: halo_copy(buffer, d, send_sems, recv_sems).wait_recv()
            )

    def halo_sent(buffer, send_sems, recv_sems):
        for d, (dl, _) in enumerate(DIRECTIONS):
            pl.when(exists(dl))(
                lambda d=d: halo_copy(buffer, d, send_sems, recv_sems).wait_send()
            )

    def fold_copy(buffer, gathered, i, k):
        return pltpu.make_async_remote_copy(
            src_ref=buffer.at[pl.ds(rows, HALO), :, own_lanes],
            dst_ref=gathered.at[lon],
            send_sem=send.at[k],
            recv_sem=recv.at[k],
            device_id={"lat": lat, "lon": lax.rem(lon + i, n_lon), "ch": me},
            device_id_type=MESH,
        )

    def several(gathered, count, k):
        whole = gathered.at[pl.ds(0, count)]
        return pltpu.make_async_remote_copy(
            src_ref=whole,
            dst_ref=whole,
            send_sem=send.at[k],
            recv_sem=recv.at[k],
            device_id={"lat": across, "lon": lon, "ch": me},
            device_id_type=MESH,
        )

    def channel_copies(make_src, dst, k, wanted=None):
        def step(j, carry):
            away = (j + 1) // 2
            peer = lax.rem(me + n_ch // 2 + n_ch + away * (1 - 2 * lax.rem(j, 2)), n_ch)

            def go():
                pltpu.make_async_remote_copy(
                    src_ref=make_src(peer),
                    dst_ref=dst,
                    send_sem=send.at[k],
                    recv_sem=recv.at[k],
                    device_id={"lat": across, "lon": lon, "ch": peer},
                    device_id_type=MESH,
                ).start()

            if wanted is None:
                go()
            else:
                pl.when(wanted(peer))(go)
            return carry

        lax.fori_loop(0, n_ch, step, 0)

    def fold_start(buffer, gathered, k):
        def step(j, carry):
            away = (j + 1) // 2
            i = n_lon // 2 + away * (1 - 2 * lax.rem(j, 2))
            fold_copy(buffer, gathered, i, k).start()
            return carry

        lax.fori_loop(0, n_lon - 1, step, 0)

    halo_start(ext, halo_send, halo_recv)

    @pl.when(lat_last)
    def _():
        fold_start(ext, fold_rows, 0)

    channel_copies(
        lambda peer: weights_send, weights.at[part, me, given], 1, lambda peer: peer != me
    )
    loads[2].wait()
    for t in range(TAPS * TAPS):
        tap = jnp.broadcast_to(kernel_ref[:, t : t + 1].astype(F32), (chans, EDGE))
        taps[0, t] = tap
        taps[1, TAPS * TAPS - 1 - t] = tap
    lane = lax.broadcasted_iota(jnp.int32, (chans, EDGE), 1)
    for table in range(2):
        for a in range(TAPS):
            for b in range(HALO):
                edge_taps[table, a * HALO + b] = jnp.where(
                    lane < EDGE // 2,
                    taps[table, a * TAPS + b],
                    taps[table, a * TAPS + b + HALO + 1],
                )

    def add_line(line, table, e, a):
        parts = [
            jnp.concatenate([taps[table, a * TAPS + b]] * (cols // EDGE), axis=1)
            * line[:, EDGE - HALO + b : EDGE - HALO + b + cols]
            for b in range(TAPS)
        ]
        acc[e - a + TAPS - 1] += ((parts[0] + parts[1]) + (parts[2] + parts[3])) + (
            (parts[4] + parts[5]) + parts[6]
        )

    def conv_own(buffer, table):
        acc[...] = jnp.zeros(acc.shape, F32)
        edge_acc[...] = jnp.zeros(edge_acc.shape, F32)
        blank = jnp.zeros((chans, EDGE), F32)

        def step(e, carry):
            own = buffer[e, :, own_lanes].astype(F32)
            line = jnp.concatenate([blank, own, blank], axis=1)
            for a in range(TAPS):
                add_line(line, table, e, a)
            return carry

        lax.fori_loop(HALO, HALO + rows, step, 0, unroll=2)

    def conv_edges(table):
        def step(e, carry):
            tile = edge_tile[e - HALO]
            left = jnp.where(lane >= EDGE // 2, tile, 0.0)
            right = jnp.where(lane < EDGE // 2, tile, 0.0)
            moved = [
                jnp.where(
                    lane < EDGE // 2,
                    pltpu.roll(left, HALO - b, 1),
                    pltpu.roll(right, EDGE - 1 - b, 1),
                )
                for b in range(HALO)
            ]
            for a in range(TAPS):
                parts = [edge_taps[table, a * HALO + b] * moved[b] for b in range(HALO)]
                edge_acc[e - a + TAPS - 1] += (parts[0] + parts[1]) + parts[2]
            return carry

        lax.fori_loop(HALO, HALO + rows, step, 0, unroll=2)

    def conv_outer(buffer, table, lines):
        for e in lines:
            line = buffer[e].astype(F32)
            for a in range(TAPS):
                if 0 <= e - a < rows:
                    add_line(line, table, e, a)

    def conv_total(start, count):
        edge = edge_acc[pl.ds(TAPS - 1 + start, count)]
        both = jnp.concatenate(
            [jnp.where(lane < EDGE // 2, edge, 0.0), jnp.where(lane < EDGE // 2, 0.0, edge)],
            axis=2,
        )
        return acc[pl.ds(TAPS - 1 + start, count)] + both

    below, above = range(HALO), range(HALO + rows, HALO + rows + HALO)
    settled = rows - HALO

    conv_own(ext, 0)

    loads[3].wait()
    masked_cot = (cot_ref[...] * mask_half[None]).reshape(cells, cols)
    cot_rows[...] = dot(to_rows, masked_cot).astype(BF16).reshape(rows, chans, cols)
    channel_copies(lambda peer: cot_rows.at[peer], cot_all.at[me], 2)

    loads[4].wait()

    full_width = n_lon * cols
    turn = partner_ref[0]
    first = lax.rem(turn - lon * cols - (cols + HALO - 1) + 2 * full_width, full_width)
    first_block = first // cols
    origin = lax.rem(turn - lon * cols + EDGE - first_block * cols + 3 * full_width, full_width)

    @pl.when(lat_last)
    def _():
        source = lax.broadcasted_iota(jnp.int32, (3 * cols, wide), 0)
        want = origin - lax.broadcasted_iota(jnp.int32, (3 * cols, wide), 1)
        want = jnp.where(want < 0, want + full_width, want)
        pick[...] = (source == want).astype(BF16)

    def fold_fill(buffer, gathered):
        found = jnp.zeros((HALO * chans, wide), F32)
        for j in range(3):
            piece = gathered[lax.rem(first_block + j, n_lon)].reshape(HALO * chans, cols)
            found = found + dot(piece, pick[j * cols : (j + 1) * cols, :])
        found = found.astype(BF16).reshape(HALO, chans, wide)
        for j in range(HALO):
            buffer[HALO + rows + j] = found[HALO - 1 - j]

    def square_copy(k):
        turn, flip = square[k]
        piece = weights.at[part, :, mine]
        return pltpu.make_async_remote_copy(
            src_ref=piece,
            dst_ref=piece,
            send_sem=square_send.at[k],
            recv_sem=square_recv.at[k],
            device_id=in_square(turn, flip),
            device_id_type=MESH,
        )

    several(weights.at[part, :, mine], n_ch - 1, 1).wait_recv()
    for k in range(len(square)):
        square_copy(k).start()
    halo_arrived(ext, halo_send, halo_recv)
    unpack_edges(0)
    conv_edges(0)
    conv_outer(ext, 0, below)
    depth_rows[pl.ds(0, settled)] = conv_total(0, settled).astype(BF16)
    channel_copies(
        lambda peer: depth_rows.at[peer], depth_all.at[me], 3, lambda peer: peer < settled
    )

    @pl.when(lat_last)
    def _():
        several(fold_rows, n_lon - 1, 0).wait_recv()
        fold_fill(ext, fold_rows)

    conv_outer(ext, 0, above)
    depth_rows[pl.ds(settled, HALO)] = conv_total(settled, HALO).astype(BF16)
    channel_copies(
        lambda peer: depth_rows.at[peer], depth_all.at[me], 3, lambda peer: peer >= settled
    )

    def swap_weights(half):
        return pltpu.make_async_remote_copy(
            src_ref=weights.at[half],
            dst_ref=weights.at[half],
            send_sem=send.at[4],
            recv_sem=recv.at[4],
            device_id={"lat": sibling, "lon": lon, "ch": me},
            device_id_type=MESH,
        )

    for k in range(len(square)):
        square_copy(k).wait_recv()
    swap_weights(part).start()
    several(cot_all, n_ch, 2).wait_recv()
    several(depth_all, n_ch, 3).wait_recv()

    channels = n_ch * chans
    values = depth_all[...].reshape(channels, cols).astype(F32)
    spread = values - jnp.mean(values, axis=0, keepdims=True)
    inv_scale = lax.rsqrt(jnp.mean(spread * spread, axis=0, keepdims=True) + EPSILON)
    normed_ref[...] = spread * inv_scale
    normed_half = normed_ref[...].astype(BF16)
    cot_here = cot_all[...].reshape(channels, cols)
    swap_weights(1 - part).wait_recv()

    back_norm = jnp.zeros((channels, cols), F32)
    per_chunk = n_ch // 4
    chunk = per_chunk * hidden_here
    chunks = [slice(j * per_chunk, (j + 1) * per_chunk) for j in range(4)]
    for j, span in enumerate(chunks):
        expand = weights[0, span].reshape(chunk, channels)
        project = weights[1, span].reshape(chunk, channels)
        active, slope = gelu_parts(dot(expand, normed_half))
        active_half[j] = active.astype(BF16)
        back_hidden = (dot(project, cot_here) * slope).astype(BF16)
        back_norm = back_norm + dot(expand, back_hidden, ((0,), (0,)))
    normed = normed_ref[...]
    mean_plain = jnp.mean(back_norm, axis=0, keepdims=True)
    mean_cross = jnp.mean(back_norm * normed, axis=0, keepdims=True)
    grad_send[...] = (
        (inv_scale * (back_norm - mean_plain - normed * mean_cross))
        .astype(BF16)
        .reshape(n_ch, chans, cols)
    )
    channel_copies(lambda peer: grad_send.at[peer], ext_back.at[HALO + me, :, own_lanes], 5)
    mixed = jnp.zeros((channels, cols), F32)
    for j, span in enumerate(chunks):
        mixed = mixed + dot(
            weights[1, span].reshape(chunk, channels), active_half[j], ((0,), (0,))
        )
    mixed_send[...] = mixed.astype(BF16).reshape(n_ch, chans, cols)

    several(grad_send, n_ch, 5).wait_recv()
    pack_edges(ext_back[own_rows, :, own_lanes].reshape(cells, cols), 1)
    halo_start(ext_back, halo_send_back, halo_recv_back)

    @pl.when(lat_last)
    def _():
        fold_start(ext_back, fold_rows_back, 7)
        fold_rows_back[lon] = ext_back[pl.ds(rows, HALO), :, own_lanes]

    channel_copies(lambda peer: mixed_send.at[peer], mixed_rows.at[me], 6)
    conv_own(ext_back, 1)
    halo_arrived(ext_back, halo_send_back, halo_recv_back)
    unpack_edges(1)
    conv_edges(1)
    conv_outer(ext_back, 1, below)
    to_chans = (swap_col == lax.rem(swap_row, rows) * chans + swap_row // rows).astype(BF16)
    several(mixed_rows, n_ch, 6).wait_recv()
    mixed_here = dot(to_chans, mixed_rows[...].reshape(cells, cols)).reshape(chans, rows, cols)
    state_sum[...] = (
        mask_ref[...].astype(F32)[None] * (state_ref[...].astype(F32) + mixed_here)
    ).astype(BF16)

    @pl.when(lat_last)
    def _():
        several(fold_rows_back, n_lon - 1, 7).wait_recv()
        fold_fill(ext_back, fold_rows_back)

    conv_outer(ext_back, jnp.where(lat_last, 0, 1), above)
    ocean = mask_ref[...].astype(F32)
    grad_rows = (
        cot_rows[...].astype(F32) + ocean[:, None, :] * conv_total(0, rows)
    ).astype(BF16)
    grad_sum[...] = (
        dot(to_chans, grad_rows.reshape(cells, cols)).astype(BF16).reshape(chans, rows, cols)
    )

    halo_sent(ext, halo_send, halo_recv)
    halo_sent(ext_back, halo_send_back, halo_recv_back)

    @pl.when(lat_last)
    def _():
        several(fold_rows, n_lon - 1, 0).wait_send()
        several(fold_rows_back, n_lon - 1, 7).wait_send()

    several(weights.at[part, :, mine], n_ch - 1, 1).wait_send()
    for k in range(len(square)):
        square_copy(k).wait_send()
    several(cot_rows, n_ch, 2).wait_send()
    several(depth_rows, n_ch, 3).wait_send()
    swap_weights(part).wait_send()
    several(grad_send, n_ch, 5).wait_send()
    several(mixed_send, n_ch, 6).wait_send()


def finish_kernel(state_sum, grad_sum, out_ref, grad_ref, sems):
    out_ref[...] = state_sum[...]
    grad_ref[...] = grad_sum[...]


def on_device(state_field, land_mask, partner, kernel, w_expand, w_project, cotangent):
    n_lat, n_lon, n_ch = (lax.axis_size(name) for name in ("lat", "lon", "ch"))
    chans, rows, cols = state_field.shape
    hidden_here = w_project.shape[0]
    assert rows == n_ch and n_lat == 4 and n_lon % 2 == 0 and cols == 2 * EDGE
    wide = cols + 2 * EDGE
    channels = n_ch * chans
    sizes = (n_lat, n_lon, n_ch, rows, chans, cols, hidden_here)
    vmem = pl.BlockSpec(memory_space=pltpu.VMEM)
    tile_rows = rows + 2 * HALO
    state_sum, grad_sum = pl.pallas_call(
        functools.partial(block_kernel, sizes),
        out_shape=(jax.ShapeDtypeStruct(state_field.shape, BF16),) * 2,
        in_specs=[pl.BlockSpec(memory_space=pltpu.HBM)] * 7,
        out_specs=(vmem, vmem),
        scratch_shapes=[
            pltpu.SMEM(partner.shape, jnp.int32),
            pltpu.VMEM(state_field.shape, BF16),
            pltpu.VMEM(land_mask.shape, jnp.int32),
            pltpu.VMEM(kernel.shape, BF16),
            pltpu.VMEM(cotangent.shape, BF16),
            pltpu.VMEM((tile_rows, chans, wide), BF16),
            pltpu.VMEM((tile_rows, chans, wide), BF16),
            pltpu.VMEM((n_lon, HALO, chans, cols), BF16),
            pltpu.VMEM((n_lon, HALO, chans, cols), BF16),
            pltpu.VMEM((3 * cols, wide), BF16),
            pltpu.VMEM((2, TAPS * TAPS, chans, EDGE), F32),
            pltpu.VMEM((rows + 2 * (TAPS - 1), chans, cols), F32),
            pltpu.VMEM((2, TAPS * HALO, chans, EDGE), F32),
            pltpu.VMEM((rows + 2 * (TAPS - 1), chans, EDGE), F32),
            pltpu.VMEM((2, 2, 2 * 8, rows * chans), BF16),
            pltpu.VMEM((2, 2, 2 * 8, rows * chans), BF16),
            pltpu.VMEM((rows, chans, EDGE), F32),
            pltpu.VMEM((rows, chans, cols), BF16),
            pltpu.VMEM((n_ch, chans, cols), BF16),
            pltpu.VMEM((rows, chans, cols), BF16),
            pltpu.VMEM((n_ch, chans, cols), BF16),
            pltpu.VMEM((2, n_ch, hidden_here, channels), BF16),
            pltpu.VMEM((hidden_here // n_lat, channels), BF16),
            pltpu.VMEM((channels, cols), F32),
            pltpu.VMEM((4, n_ch // 4 * hidden_here, cols), BF16),
            pltpu.VMEM((n_ch, chans, cols), BF16),
            pltpu.VMEM((n_ch, chans, cols), BF16),
            pltpu.VMEM((n_ch, chans, cols), BF16),
            pltpu.SemaphoreType.DMA((8,)),
            pltpu.SemaphoreType.DMA((8,)),
            pltpu.SemaphoreType.DMA((8,)),
            pltpu.SemaphoreType.DMA((8,)),
            pltpu.SemaphoreType.DMA((8,)),
            pltpu.SemaphoreType.DMA((8,)),
            pltpu.SemaphoreType.DMA((n_lat - 1,)),
            pltpu.SemaphoreType.DMA((n_lat - 1,)),
            pltpu.SemaphoreType.DMA((7,)),
        ],
        compiler_params=pltpu.CompilerParams(
            collective_id=0, has_side_effects=True, vmem_limit_bytes=64 * 1000 * 1000
        ),
        name="ocean_block",
    )(partner, state_field, land_mask, kernel, w_expand.T, w_project, cotangent)
    anywhere = pl.BlockSpec(memory_space=pltpu.VMEM)
    return pl.pallas_call(
        finish_kernel,
        out_shape=(jax.ShapeDtypeStruct(state_field.shape, BF16),) * 2,
        in_specs=[anywhere] * 2,
        out_specs=(anywhere, anywhere),
        scratch_shapes=[pltpu.SemaphoreType.DMA((2,))],
        name="finish",
    )(state_sum, grad_sum)


def solution(mesh):
    placed = (
        P("ch", "lat", "lon"),
        P("lat", "lon"),
        P(),
        P("ch", None),
        P(None, "ch"),
        P("ch", None),
        P("ch", "lat", "lon"),
    )
    return jax.shard_map(
        on_device,
        mesh=mesh,
        in_specs=placed,
        out_specs=(P("ch", "lat", "lon"), P("ch", "lat", "lon")),
        check_vma=False,
    )
```
